128 devices in a mesh: ingest: 4 (over x), owner: 32 (over y, z, core).
Axes of the slice: x: 4, y: 4, z: 4, core: 2. Of those that a mesh axis runs over, the one named last changes fastest.
Arguments:
- frame_mel: bfloat16 [131072, 48], P(('ingest', 'owner')), may hold values from -6 to 6
- row_device: int32 [131072, 1], P(('ingest', 'owner')), may hold values from 0 to 127; in each aligned block of 1024 rows (0 to 1023, 1024 to 2047, ...) at most 11 rows name the same one
- row_slot: int32 [131072], P(('ingest', 'owner')), may hold values from 0 to 3
- window_length: int32 [512], replicated, may hold values from 2 to 512, as said below
- migrate_count: int32 [128], replicated, may hold values from 0 to 2, as said below
- conv_state: bfloat16 [512, 256], P(('ingest', 'owner')), may hold values from -6 to 6
- kv_cache: bfloat16 [512, 2, 512, 256], P(('ingest', 'owner'))
- w_in: bfloat16 [48, 256], replicated, may hold values from -0.875 to 0.875
- w_state: bfloat16 [256, 256], replicated, may hold values from -0.375 to 0.375
- w_qkv: bfloat16 [256, 768], replicated, may hold values from -0.375 to 0.375
- w_out: bfloat16 [256, 256], replicated, may hold values from -0.375 to 0.375
Outputs:
- frame_scores: bfloat16 [131072, 256], P(('ingest', 'owner'))
- new_state: bfloat16 [768, 256], P(('ingest', 'owner'))
The draws below stay inside these ranges and needn't reach their ends.
Inputs may be any that keep to these rules, and one draw needn't show every extreme that they name: `row_device`: no device is named by more than 11 rows of one device; some device reaches it. `window_length`: the first session of every device has 512 valid frames. `migrate_count`: a device's migrated sessions are its highest slots; some device moves 2.
All inputs are finite; a program needn't handle non-finite values.
Results may differ from the reference program's by a relative error of at most 0.0087.
Values may be sent and summed in bfloat16 or wider, within the bound.
A program may use at most 64 MiB of HBM per device.

```python
import math
import jax
import jax.numpy as jnp
import numpy as np
from jax import lax

MEL = 48
C = 256
HEADS = 4
HEAD_DIM = 64
WIN = 512
ROWS_DEV = 1024
SESS_DEV = 4
MIG = 2
SLOTS = 6
CAP = 11
ROWS = 131072
SESSIONS = 512
N_OWNER = 32
DEVICES = 128


def draw_window_length(key, part):
    values = jax.random.randint(key, (SESSIONS,), 2, WIN + 1, dtype=jnp.int32)
    return values.at[::SESS_DEV].set(WIN)


def draw_migrate_count(key, part):
    values = jax.random.randint(key, (DEVICES,), 0, MIG + 1, dtype=jnp.int32)
    return values.at[0].set(MIG)


def draw_kv_cache(key, part):
    base = jax.random.normal(key, (SESSIONS, 2, WIN, C), jnp.float32)
    return base.astype(jnp.bfloat16)


def with_ends(result, stream_key, smallest, largest):
    extent = result.shape
    index_at = [jax.random.randint(jax.random.fold_in(stream_key, axis), (), 0, extent[axis]) for axis in range(len(extent))]
    result = result.at[tuple(index_at)].set(smallest)
    longest = extent.index(max(extent))
    index_at[longest] = (index_at[longest] + 1) % extent[longest]
    return result.at[tuple(index_at)].set(largest)


def block_levels(own_key, dims, split, smallest, largest):
    level = 1.0
    for dim, shards_of in split:
        steps = jax.random.uniform(jax.random.fold_in(jax.random.fold_in(own_key, 6), dim), (shards_of,), jnp.float32, smallest / len(split), largest / len(split))
        level = level * jnp.repeat(jnp.exp(steps), dims[dim] // shards_of).reshape((-1,) + (1,) * (len(dims) - 1 - dim))
    return level


def deal_out(rng, own, number, rows, number_of, top, most, lean):
    sequence = jax.random.permutation(rng, number_of)
    packed, common = load_shares(number_of, rows * top, most, lean, True), load_shares(number_of, rows * top, most, lean, False)
    places = jnp.arange(number_of)

    def named(sizes, offset_by):
        used = int((sizes > 0).sum())
        fixed = max(1, used // 4)
        shifted = fixed + (places - fixed + offset_by * (used - fixed)) % max(1, number_of - fixed)
        return jnp.zeros((number_of,), jnp.int32).at[sequence[jnp.where(places < fixed, places, shifted)]].set(jnp.asarray(sizes, jnp.int32))

    sizes = jnp.where(number % 4 == 0, named(packed, number // 4), named(common, number - number // 4 - 1))
    mixed = jax.random.permutation(jax.random.fold_in(own, 3), number_of)
    donor, taker = mixed[0:number_of // 2 * 2:2], mixed[1:number_of // 2 * 2:2]
    margin = jnp.minimum(sizes[donor] - 1, most - sizes[taker]) // 2
    margin = jnp.where((donor == sequence[0]) | (taker == sequence[0]) | (sizes[taker] == 0), 0, jnp.maximum(margin, 0))
    shifted = jax.random.randint(jax.random.fold_in(own, 4), (number_of // 2,), 0, 1 << 20) % (margin + 1)
    sizes = sizes.at[donor].add(-shifted).at[taker].add(shifted)
    labels = jnp.searchsorted(jnp.cumsum(sizes), jnp.arange(rows * top), side="right").astype(jnp.int32)
    table = labels.reshape(top, rows).T
    table = table[jax.random.permutation(jax.random.fold_in(own, 1), rows)]
    offset_by = jax.random.randint(jax.random.fold_in(own, 2), (rows, 1), 0, top)
    return jnp.take_along_axis(table, (jnp.arange(top)[None, :] + offset_by) % top, axis=1)


def load_shares(count, total, bound, lean, full):
    portions = [(1 << 20) // math.isqrt(grade ** lean) + 1 for grade in range(1, count + 1)]
    largest = bound if full else min(bound, max(-(-total // count), total * portions[0] // sum(portions)))
    least = 1 if total - largest >= count - 1 else 0
    given, spare = [largest] + [least] * (count - 1), total - largest - least * (count - 1)
    while spare > 0:
        free = [i for i in range(1, count) if given[i] < largest] or [i for i in range(1, count) if given[i] < bound]
        pool, remaining = sum([portions[i] for i in free]), spare
        for i in free:
            addition = min(bound - given[i], max(1, remaining * portions[i] // pool), spare)
            given[i] = given[i] + addition
            spare = spare - addition
    return np.array(given)


def normal_values(rng, shape, spread, bound, cuts=(), kind=jnp.bfloat16):
    values = spread * jax.random.normal(rng, shape, jnp.float32)
    if cuts:
        values = values * block_levels(rng, shape, cuts, -0.22, 0.18)
    return jnp.clip(values, -bound, bound).astype(kind)


def setup_inputs(seed: int = 0) -> dict:
    streams_of = jax.random.split(jax.random.key(seed), 12)
    frame_mel = normal_values(streams_of[0], (ROWS, MEL), 1.0, 6.0, ((0, 128),))
    row_device_keys = jax.random.split(jax.random.fold_in(streams_of[1], 1), ROWS // ROWS_DEV)
    row_device_turns = jax.random.permutation(jax.random.fold_in(streams_of[1], 3), ROWS // ROWS_DEV)
    row_device = jax.vmap(lambda own, number: deal_out(jax.random.fold_in(streams_of[1], 2), own, number, ROWS_DEV, DEVICES, 1, CAP, 2))(row_device_keys, row_device_turns).reshape((ROWS, 1))
    row_slot = with_ends(jax.random.randint(streams_of[2], (ROWS,), 0, SESS_DEV), jax.random.fold_in(streams_of[2], 1), 0, SESS_DEV - 1).astype(jnp.int32)
    window_length = draw_window_length(jax.random.fold_in(streams_of[11], 71), 0)
    migrate_count = draw_migrate_count(jax.random.fold_in(streams_of[11], 71), 0)
    conv_state = normal_values(streams_of[5], (SESSIONS, C), 1.0, 6.0, ((0, 128),))
    kv_cache = draw_kv_cache(jax.random.fold_in(streams_of[11], 71), 0)
    w_in = normal_values(streams_of[7], (MEL, C), MEL ** -0.5, 0.875)
    w_state = normal_values(streams_of[8], (C, C), C ** -0.5, 0.375)
    w_qkv = normal_values(streams_of[9], (C, 3 * C), C ** -0.5, 0.375)
    w_out = normal_values(streams_of[10], (C, C), C ** -0.5, 0.375)
    return {"frame_mel": frame_mel, "row_device": row_device, "row_slot": row_slot, "window_length": window_length, "migrate_count": migrate_count, "conv_state": conv_state, "kv_cache": kv_cache, "w_in": w_in, "w_state": w_state, "w_qkv": w_qkv, "w_out": w_out}


def attend_block(q4, k4, v4, keys, values, length):
    scale = HEAD_DIM ** -0.5
    qf = q4.astype(jnp.float32)
    score = jnp.einsum("bhd,phd->bhp", qf, keys.astype(jnp.float32)) * scale
    valid = jnp.arange(WIN, dtype=jnp.int32) < length
    score = jnp.where(valid[None, None, :], score, -1e30)
    own = jnp.sum(qf * k4.astype(jnp.float32), axis=-1) * scale
    top = jnp.maximum(jnp.max(score, axis=-1), own)
    expo = jnp.exp(score - top[..., None])
    own_exp = jnp.exp(own - top)
    total = jnp.sum(expo, axis=-1) + own_exp
    weights = (expo / total[..., None]).astype(jnp.bfloat16)
    own_weight = (own_exp / total).astype(jnp.bfloat16)
    mixed = jnp.einsum("bhp,phd->bhd", weights.astype(jnp.float32), values.astype(jnp.float32))
    mixed = mixed + own_weight.astype(jnp.float32)[..., None] * v4.astype(jnp.float32)
    return mixed.reshape(q4.shape[0], C).astype(jnp.bfloat16)


def reference(frame_mel, row_device, row_slot, window_length, migrate_count, conv_state, kv_cache, w_in, w_state, w_qkv, w_out):
    feats = jnp.dot(frame_mel, w_in, preferred_element_type=jnp.float32).astype(jnp.bfloat16)
    session = (row_device[:, 0] * SESS_DEV + row_slot).astype(jnp.int32)
    carried = jnp.dot(conv_state, w_state, preferred_element_type=jnp.float32)
    hidden = jax.nn.silu(feats.astype(jnp.float32) + carried[session]).astype(jnp.bfloat16)
    qkv = jnp.dot(hidden, w_qkv, preferred_element_type=jnp.float32).astype(jnp.bfloat16)
    order = jnp.argsort(session).astype(jnp.int32)
    counts_int = jax.ops.segment_sum(jnp.ones((ROWS,), jnp.int32), session, SESSIONS).astype(jnp.int32)
    row_starts = (jnp.cumsum(counts_int) - counts_int).astype(jnp.int32)
    spans = ((counts_int + 63) // 64).astype(jnp.int32)
    block_ends = jnp.cumsum(spans).astype(jnp.int32)
    block_starts = (block_ends - spans).astype(jnp.int32)
    sorted_sess = session[order]
    rank = (jnp.arange(ROWS, dtype=jnp.int32) - row_starts[sorted_sess]).astype(jnp.int32)
    place_sorted = (block_starts[sorted_sess] * 64 + rank).astype(jnp.int32)
    place = jnp.zeros((ROWS,), jnp.int32).at[order].set(place_sorted)
    block_total = ROWS // 64 + SESSIONS
    padded = jnp.zeros((block_total * 64, 3 * C), jnp.bfloat16).at[place].set(qkv)
    block_ids = jnp.arange(block_total, dtype=jnp.int32)
    block_session = jnp.sum((block_ends[None, :] <= block_ids[:, None]).astype(jnp.int32), axis=1).astype(jnp.int32)
    block_session = jnp.minimum(block_session, SESSIONS - 1).astype(jnp.int32)

    def one_block(index):
        taken = lax.dynamic_slice_in_dim(padded, index * 64, 64, 0)
        which = block_session[index]
        cache = lax.dynamic_index_in_dim(kv_cache, which, 0, keepdims=False)
        q4 = taken[:, :C].reshape(64, HEADS, HEAD_DIM)
        k4 = taken[:, C:2 * C].reshape(64, HEADS, HEAD_DIM)
        v4 = taken[:, 2 * C:].reshape(64, HEADS, HEAD_DIM)
        keys = cache[0].reshape(WIN, HEADS, HEAD_DIM)
        values = cache[1].reshape(WIN, HEADS, HEAD_DIM)
        return attend_block(q4, k4, v4, keys, values, window_length[which])

    blocks_out = lax.map(one_block, block_ids).reshape(block_total * 64, C)
    attn = blocks_out[place]
    frame_scores = (hidden.astype(jnp.float32) + jnp.dot(attn, w_out, preferred_element_type=jnp.float32)).astype(jnp.bfloat16)
    sums = jax.ops.segment_sum(frame_scores.astype(jnp.float32), session, SESSIONS)
    counts = jax.ops.segment_sum(jnp.ones((ROWS,), jnp.float32), session, SESSIONS)
    mean = sums / jnp.maximum(counts, 1.0)[:, None]
    updated = jnp.where(counts[:, None] > 0, mean, conv_state.astype(jnp.float32)).astype(jnp.bfloat16)
    table = updated.reshape(DEVICES, SESS_DEV, C)
    device_ids = jnp.arange(DEVICES, dtype=jnp.int32)
    before = (device_ids // N_OWNER) * N_OWNER + (device_ids % N_OWNER + N_OWNER - 1) % N_OWNER
    keep = jnp.arange(SESS_DEV, dtype=jnp.int32)[None, :] < (SESS_DEV - migrate_count)[:, None]
    own_part = jnp.where(keep[..., None], table, jnp.zeros_like(table))
    incoming = table[before][:, SESS_DEV - MIG:, :]
    live = jnp.arange(MIG, dtype=jnp.int32)[None, :] >= (MIG - migrate_count[before])[:, None]
    in_part = jnp.where(live[..., None], incoming, jnp.zeros_like(incoming))
    new_state = jnp.concatenate([own_part, in_part], axis=1).reshape(DEVICES * SLOTS, C)
    return frame_scores, new_state
```

```python
import functools

import jax
import jax.numpy as jnp
from jax import lax
from jax.experimental import pallas as pl
from jax.experimental.pallas import tpu as pltpu
from jax.sharding import PartitionSpec as P

HEADS = 4
MIG = 2
MESH = pl.DeviceIdType.MESH
F32 = jnp.float32
BF16 = jnp.bfloat16
I32 = jnp.int32


def iota(shape, dim):
    return lax.broadcasted_iota(I32, shape, dim)


def one_hot(mask):
    return jnp.where(mask, 1.0, 0.0).astype(BF16)


def mm(a, b):
    return jnp.dot(a, b, preferred_element_type=F32)


def kernel(
    n_ing,
    n_own,
    G,
    dev_ref,
    slot_ref,
    lens_ref,
    mig_ref,
    conv_ref,
    mel_ref,
    kv_ref,
    w_in_ref,
    w_state_ref,
    w_qkv_ref,
    w_out_ref,
    out_ref,
    new_ref,
    snd,
    rcv,
    rsnd,
    ret,
    kvb,
    kt,
    vc,
    mel2,
    um,
    ue,
    wx,
    sums,
    counts,
    upd_out,
    upd_in,
    kv_sem,
    ssem,
    rsem,
    bsem,
    csem,
    usem,
):
    devices = n_ing * n_own
    groups = devices // G
    rows = mel_ref.shape[1]
    mel = mel_ref.shape[0]
    sess, width = conv_ref.shape
    window = kv_ref.shape[2]
    ing = lax.axis_index("ingest")
    own = lax.axis_index("owner")
    me = ing * n_own + own
    grp = me // G

    def coords(p):
        return (p // n_own, p % n_own)

    kv_copy = pltpu.make_async_copy(kv_ref, kvb, kv_sem)
    kv_copy.start()

    barrier = pltpu.get_barrier_semaphore()

    def greet(i, c):
        p = lax.rem(me + i, devices)
        pl.semaphore_signal(barrier, inc=1, device_id=coords(p), device_id_type=MESH)
        return c

    lax.fori_loop(1, devices, greet, 0)

    dev = dev_ref[...]
    slot = slot_ref[...]
    step = 256
    upper = one_hot(iota((step, step), 0) < iota((step, step), 1))
    lane_dev = iota((devices, step), 0)
    carry = jnp.zeros((devices, 1), F32)
    ranks = []
    for b in range(rows // step):
        hit = jnp.where(lane_dev == dev[:, b * step : (b + 1) * step], 1.0, 0.0)
        before = mm(hit.astype(BF16), upper) + carry
        ranks.append(jnp.sum(before * hit, axis=0, keepdims=True))
        carry = carry + jnp.sum(hit, axis=1, keepdims=True)
    rank = jnp.concatenate(ranks, axis=1).astype(I32)
    code0 = jnp.where(rank < 8, dev * 8 + rank, -1)
    code1 = jnp.where(rank >= 8, dev * 8 + rank - 8, -1)
    code2 = jnp.where(rank >= 8, dev * 4 + rank - 8, -1)

    r16 = iota((16, rows), 0)
    slots = one_hot((r16 % 4 == slot) & (r16 < 12))
    half = jnp.concatenate([mel_ref[...], slots], axis=0)
    mel2[...] = jnp.concatenate([half, half], axis=0).T

    pl.semaphore_wait(barrier, devices - 1)

    tile = G * 8
    low = iota((tile, 128), 1) < 64

    def pack(j, c):
        g = lax.rem(grp + j, groups)
        at = iota((tile, rows), 0) + g * tile
        mels = mel2[...]
        first = mm(one_hot(at == code0), mels)
        second = mm(one_hot(at == code1), mels)
        packed = jnp.where(low, first, second).astype(BF16)
        snd[pl.ds(g * G, G)] = packed.reshape(G, 8, 128)

        def send(i, c):
            p = g * G + lax.rem(me + i, G)

            @pl.when(p != me)
            def _():
                pltpu.make_async_remote_copy(
                    src_ref=snd.at[p],
                    dst_ref=rcv.at[me],
                    send_sem=ssem,
                    recv_sem=rsem.at[grp],
                    device_id=coords(p),
                    device_id_type=MESH,
                ).start()

            return c

        lax.fori_loop(0, G, send, 0)
        return c

    lax.fori_loop(0, groups, pack, 0)
    rcv[pl.ds(me, 1)] = snd[pl.ds(me, 1)]

    r4 = iota((16, width), 0)
    states = mm(conv_ref[...], w_state_ref[...])
    tiled = jnp.zeros((16, width), F32)
    for s in range(sess):
        tiled = jnp.where(r4 % 4 == s, states[s : s + 1, :], tiled)
    hi = tiled.astype(BF16).astype(F32)
    mid = (tiled - hi).astype(BF16).astype(F32)
    lo = tiled - hi - mid
    terms = jnp.where(r4 < 4, hi, jnp.where(r4 < 8, mid, jnp.where(r4 < 12, lo, 0.0)))
    lanes4 = jnp.where((iota((16, width), 1) // 64 == r4) & (r4 < 4), 1.0, 0.0)
    r16l = iota((16, 128), 0)
    length = jnp.zeros((16, 128), I32)
    for s in range(sess):
        length = jnp.where(r16l % 4 == s, lens_ref[me * sess + s], length)
    length = jnp.where(
        r16l < 4, (length // 256) * 256, jnp.where(r16l < 8, length % 256, 0)
    ).astype(F32)
    wx[...] = jnp.zeros_like(wx)
    wx[0:mel, 0:width] = w_in_ref[...]
    wx[mel : mel + 16, :] = jnp.concatenate([terms, lanes4, length], axis=1).astype(BF16)

    kv_copy.wait()
    low_p = iota((window, 128), 1) < 64
    for pair in range(HEADS // 2):
        cols = slice(pair * 128, pair * 128 + 128)
        for sp in range(2):
            there = slice(sp * 128, sp * 128 + 128)
            for which in range(2):
                one = kvb[2 * sp, which, :, cols].astype(F32)
                two = kvb[2 * sp + 1, which, :, cols].astype(F32)
                even = jnp.where(low_p, one, pltpu.roll(two, 64, 1)).astype(BF16)
                odd = jnp.where(low_p, pltpu.roll(one, 64, 1), two).astype(BF16)
                if which == 0:
                    kt[2 * pair, there, :] = even.T
                    kt[2 * pair + 1, there, :] = odd.T
                else:
                    vc[2 * pair, :, there] = even
                    vc[2 * pair + 1, :, there] = odd

    diag = iota((128, 128), 0) == iota((128, 128), 1)
    for b in range(rows // 128):
        here = slice(b * 128, b * 128 + 128)
        c0 = jnp.sum(jnp.where(diag, code0[:, here].astype(F32), 0.0), axis=1, keepdims=True)
        c2 = jnp.sum(jnp.where(diag, code2[:, here].astype(F32), 0.0), axis=1, keepdims=True)
        um[here, :] = one_hot(iota((128, devices * 8), 1) == c0.astype(I32))
        ue[here, :] = one_hot(iota((128, devices * 4), 1) == c2.astype(I32))

    total = 12 * G
    sums[...] = jnp.zeros_like(sums)
    counts[...] = jnp.zeros_like(counts)
    pick = one_hot(
        (iota((4 * G, 8 * G), 0) // 4 == iota((4 * G, 8 * G), 1) // 8)
        & (iota((4 * G, 8 * G), 0) % 4 == iota((4 * G, 8 * G), 1) % 8)
    )
    slot_lane = one_hot((iota((8, 128), 1) == iota((8, 128), 0) + mel) & (iota((8, 128), 0) < sess))
    low_r = iota((total, 128), 1) < 64
    position = iota((total, window), 1)
    sub = iota((G // 2, 8, 128), 1) < 4

    def score(j, c):
        g = lax.rem(grp - j + groups, groups)

        @pl.when(j == 0)
        def _():
            part = rcv.at[pl.ds(g * G, G - 1)]
            pltpu.make_async_copy(part, part, rsem.at[g]).wait()

        @pl.when(j > 0)
        def _():
            part = rcv.at[pl.ds(g * G, G)]
            pltpu.make_async_copy(part, part, rsem.at[g]).wait()

        a = rcv[pl.ds(g * G, G)].reshape(8 * G, 128)
        x = pltpu.roll(mm(pick, a), 64, 1).astype(BF16)
        both = jnp.concatenate([a, x], axis=0)
        f = mm(both, wx[...])
        pre = f[:, :width]
        mask4 = f[:, width : 2 * width]
        valid = position < f[:, 2 * width : 2 * width + 1].astype(I32)
        hidden = (pre * jax.nn.sigmoid(pre)).astype(BF16)
        qkv = mm(hidden, w_qkv_ref[...])
        outs = []
        for pair in range(HEADS // 2):
            cols = slice(pair * 128, pair * 128 + 128)
            q = qkv[:, pair * 128 : pair * 128 + 128].astype(BF16).astype(F32) * 0.125
            k = qkv[:, width + pair * 128 : width + pair * 128 + 128].astype(BF16).astype(F32)
            v = qkv[:, 2 * width + pair * 128 : 2 * width + pair * 128 + 128]
            v = v.astype(BF16).astype(F32)
            turned = pltpu.roll(q, 64, 1)
            halves = (jnp.where(low_r, q, turned), jnp.where(low_r, turned, q))
            mixed, tops, totals = [], [], []
            for h in range(2):
                wide = (jnp.concatenate([halves[h], halves[h]], axis=1) * mask4).astype(BF16)
                s = jnp.where(valid, mm(wide, kt[2 * pair + h]), -1e30)
                top = jnp.max(s, axis=1, keepdims=True)
                e = jnp.exp(s - top)
                totals.append(jnp.sum(e, axis=1, keepdims=True))
                tops.append(top)
                o = mm(e.astype(BF16), vc[2 * pair + h]) * mask4
                mixed.append(o[:, :128] + o[:, 128:])
            mix = jnp.where(low_r, mixed[0], mixed[1]) + pltpu.roll(
                jnp.where(low_r, mixed[1], mixed[0]), 64, 1
            )
            top = jnp.where(low_r, tops[0], tops[1])
            tot = jnp.where(low_r, totals[0], totals[1])
            prod = q * k
            own0 = jnp.sum(jnp.where(low_r, prod, 0.0), axis=1, keepdims=True)
            own1 = jnp.sum(jnp.where(low_r, 0.0, prod), axis=1, keepdims=True)
            mine = jnp.where(low_r, own0, own1)
            peak = jnp.maximum(top, mine)
            ea = jnp.exp(top - peak)
            eb = jnp.exp(mine - peak)
            outs.append(((ea * mix + eb * v) / (ea * tot + eb)).astype(BF16))
        attn = jnp.concatenate(outs, axis=1)
        scored = (hidden.astype(F32) + mm(attn, w_out_ref[...])).astype(BF16)
        wide = scored.astype(F32)
        first = pl.ds(g * G, G)
        rsnd[first, 0:8, :] = scored[: 8 * G, :128].reshape(G, 8, 128)
        rsnd[first, 8:16, :] = scored[: 8 * G, 128:].reshape(G, 8, 128)
        left = wide[8 * G :, :128].reshape(G // 2, 8, 128)
        right = wide[8 * G :, 128:].reshape(G // 2, 8, 128)
        ones = jnp.where(sub, left, pltpu.roll(right, 4, 1))
        twos = jnp.where(sub, pltpu.roll(left, 4, 1), right)
        rsnd[first, 16:24, :] = jnp.stack([ones, twos], axis=1).reshape(G, 8, 128).astype(BF16)

        def back(i, c):
            p = g * G + lax.rem(me + i, G)

            @pl.when(p != me)
            def _():
                pltpu.make_async_remote_copy(
                    src_ref=rsnd.at[p],
                    dst_ref=ret.at[me],
                    send_sem=bsem,
                    recv_sem=csem,
                    device_id=coords(p),
                    device_id_type=MESH,
                ).start()

            return c

        lax.fori_loop(0, G, back, 0)
        marks = lax.dot_general(
            slot_lane, both, (((1,), (1,)), ((), ())), preferred_element_type=F32
        )
        sums[...] += mm(marks.astype(BF16), scored)
        counts[...] += jnp.sum(marks, axis=1, keepdims=True)
        return c

    lax.fori_loop(0, groups, score, 0)
    ret[pl.ds(me, 1)] = rsnd[pl.ds(me, 1)]

    n = counts[0:sess, 0:1]
    mean = sums[0:sess, :] / jnp.maximum(n, 1.0)
    updated = jnp.where(n > 0, mean, conv_ref[...].astype(F32)).astype(BF16).astype(F32)
    upd_out[...] = jnp.zeros_like(upd_out)
    upd_out[0:sess, :] = updated
    push = pltpu.make_async_remote_copy(
        src_ref=upd_out,
        dst_ref=upd_in,
        send_sem=usem.at[0],
        recv_sem=usem.at[1],
        device_id=(ing, lax.rem(own + 1, n_own)),
        device_id_type=MESH,
    )
    push.start()
    push.wait()
    r8 = iota((8, width), 0)
    prev = ing * n_own + lax.rem(own + n_own - 1, n_own)
    keep = (r8 < sess) & (r8 < sess - mig_ref[me])
    live = (r8 >= sess) & (r8 - sess >= MIG - mig_ref[prev])
    table = jnp.where(
        keep, upd_out[...], jnp.where(live, pltpu.roll(upd_in[...], MIG, 0), 0.0)
    ).astype(BF16)
    new_ref[...] = table[0 : sess + MIG, :]

    other = snd.at[pl.ds(0, devices - 1)]
    pltpu.make_async_copy(other, other, ssem).wait()
    other = rsnd.at[pl.ds(0, devices - 1)]
    pltpu.make_async_copy(other, other, bsem).wait()
    other = ret.at[pl.ds(0, devices - 1)]
    pltpu.make_async_copy(other, other, csem).wait()
    main = jnp.concatenate(
        [
            ret[:, 0:8, :].reshape(devices * 8, 128),
            ret[:, 8:16, :].reshape(devices * 8, 128),
        ],
        axis=1,
    )
    extra = ret[:, 16:24, :].astype(F32).reshape(devices // 2, 2, 8, 128)
    ones, twos = extra[:, 0], extra[:, 1]
    sub = iota((devices // 2, 8, 128), 1) < 4
    left = jnp.where(sub, ones, pltpu.roll(twos, 4, 1)).reshape(devices * 4, 128)
    right = jnp.where(sub, pltpu.roll(ones, 4, 1), twos).reshape(devices * 4, 128)
    extra = jnp.concatenate([left, right], axis=1).astype(BF16)
    for b in range(rows // 256):
        here = slice(b * 256, b * 256 + 256)
        out_ref[here, :] = (mm(um[here, :], main) + mm(ue[here, :], extra)).astype(BF16)


def body(
    frame_mel,
    row_device,
    row_slot,
    window_length,
    migrate_count,
    conv_state,
    kv_cache,
    w_in,
    w_state,
    w_qkv,
    w_out,
):
    n_ing = lax.axis_size("ingest")
    n_own = lax.axis_size("owner")
    devices = n_ing * n_own
    rows, mel = frame_mel.shape
    sess, _, window, width = kv_cache.shape
    G = 16
    groups = devices // G
    vmem = pl.BlockSpec(memory_space=pltpu.VMEM)
    smem = pl.BlockSpec(memory_space=pltpu.SMEM)
    return pl.pallas_call(
        functools.partial(kernel, n_ing, n_own, G),
        out_shape=(
            jax.ShapeDtypeStruct((rows, width), BF16),
            jax.ShapeDtypeStruct((sess + MIG, width), BF16),
        ),
        in_specs=[
            vmem,
            vmem,
            smem,
            smem,
            vmem,
            vmem,
            pl.BlockSpec(memory_space=pl.ANY),
            vmem,
            vmem,
            vmem,
            vmem,
        ],
        out_specs=(vmem, vmem),
        scratch_shapes=[
            pltpu.VMEM((devices, 8, 128), BF16),
            pltpu.VMEM((devices, 8, 128), BF16),
            pltpu.VMEM((devices, 24, 128), BF16),
            pltpu.VMEM((devices, 24, 128), BF16),
            pltpu.VMEM(kv_cache.shape, BF16),
            pltpu.VMEM((HEADS, width, window), BF16),
            pltpu.VMEM((HEADS, window, width), BF16),
            pltpu.VMEM((rows, 128), BF16),
            pltpu.VMEM((rows, devices * 8), BF16),
            pltpu.VMEM((rows, devices * 4), BF16),
            pltpu.VMEM((128, 2 * width + 128), BF16),
            pltpu.VMEM((8, width), F32),
            pltpu.VMEM((8, 128), F32),
            pltpu.VMEM((8, width), F32),
            pltpu.VMEM((8, width), F32),
            pltpu.SemaphoreType.DMA,
            pltpu.SemaphoreType.DMA,
            pltpu.SemaphoreType.DMA((groups,)),
            pltpu.SemaphoreType.DMA,
            pltpu.SemaphoreType.DMA,
            pltpu.SemaphoreType.DMA((2,)),
        ],
        compiler_params=pltpu.CompilerParams(
            collective_id=0, has_side_effects=True, vmem_limit_bytes=56 << 20
        ),
        name="scorer",
    )(
        row_device.reshape(1, rows),
        row_slot.reshape(1, rows),
        window_length,
        migrate_count,
        conv_state,
        frame_mel.T,
        kv_cache,
        w_in,
        w_state,
        w_qkv,
        w_out,
    )


def solution(mesh):
    placed = (
        P(("ingest", "owner"), None),
        P(("ingest", "owner"), None),
        P(("ingest", "owner")),
        P(),
        P(),
        P(("ingest", "owner"), None),
        P(("ingest", "owner"), None, None, None),
        P(),
        P(),
        P(),
        P(),
    )
    return jax.shard_map(
        body,
        mesh=mesh,
        in_specs=placed,
        out_specs=(P(("ingest", "owner"), None), P(("ingest", "owner"), None)),
        check_vma=False,
    )
```

```python
import functools

import jax
import jax.numpy as jnp
from jax import lax
from jax.experimental import pallas as pl
from jax.experimental.pallas import tpu as pltpu
from jax.sharding import PartitionSpec as P

HEADS = 4
MIG = 2
MESH = pl.DeviceIdType.MESH
F32 = jnp.float32
BF16 = jnp.bfloat16
I32 = jnp.int32


def iota(shape, dim):
    return lax.broadcasted_iota(I32, shape, dim)


def one_hot(mask):
    return jnp.where(mask, 1.0, 0.0).astype(BF16)


def mm(a, b):
    return jnp.dot(a, b, preferred_element_type=F32)


def kernel(
    n_ing,
    n_own,
    G,
    dev_ref,
    slot_ref,
    lens_ref,
    mig_ref,
    conv_ref,
    mel_ref,
    kv_ref,
    w_in_ref,
    w_state_ref,
    w_qkv_ref,
    w_out_ref,
    out_ref,
    new_ref,
    snd,
    rcv,
    rsnd,
    ret,
    kvb,
    kt,
    vc,
    mel2,
    um,
    ue,
    wx,
    wq,
    sums,
    counts,
    upd_out,
    upd_in,
    acc,
    kv_sem,
    ssem,
    rsem,
    bsem,
    csem,
    usem,
):
    devices = n_ing * n_own
    groups = devices // G
    rows = mel_ref.shape[1]
    mel = mel_ref.shape[0]
    sess, width = conv_ref.shape
    window = kv_ref.shape[2]
    ing = lax.axis_index("ingest")
    own = lax.axis_index("owner")
    me = ing * n_own + own

    N = n_ing
    yy, zz, core = own // (2 * N), (own // 2) % N, own % 2
    mine_k = (ing + yy + zz) % N
    place = mine_k * G + ing * (2 * N) + yy * 2 + core

    def peer(k, dx, dy, dc):
        x, y, c = (ing + dx) % N, (yy + dy) % N, (core + dc) % 2
        z = (k + 2 * N - x - y) % N
        return k * G + x * (2 * N) + y * 2 + c, (x, y * (2 * N) + z * 2 + c)

    def each_peer(j, k, start):
        def step(dx, c):
            for dy in range(N):
                for dc in range(2):
                    if dy + dc > 0:
                        start(*peer(k, dx, dy, dc))
            return c

        lax.fori_loop(0, N, step, 0)
        for dx in range(1, N):
            start(*peer(k, dx, 0, 0))

        @pl.when(j > 0)
        def _():
            start(*peer(k, 0, 0, 0))

    kv_copy = pltpu.make_async_copy(kv_ref, kvb, kv_sem)
    kv_copy.start()

    barrier = pltpu.get_barrier_semaphore()

    def greet(i, c):
        for a in range(n_ing):
            x = lax.rem(ing + a, n_ing)
            y = lax.rem(own + i, n_own)
            pl.semaphore_signal(barrier, inc=1, device_id=(x, y), device_id_type=MESH)
        return c

    lax.fori_loop(1, n_own, greet, 0, unroll=4)
    for a in range(1, n_ing):
        x = lax.rem(ing + a, n_ing)
        pl.semaphore_signal(barrier, inc=1, device_id=(x, own), device_id_type=MESH)

    dev = dev_ref[...]
    slot = slot_ref[...]
    step = 256
    upper = one_hot(iota((step, step), 0) < iota((step, step), 1))
    lane_dev = iota((devices, step), 0)
    carry = jnp.zeros((devices, 1), F32)
    ranks = []
    for b in range(rows // step):
        hit = jnp.where(lane_dev == dev[:, b * step : (b + 1) * step], 1.0, 0.0)
        before = mm(hit.astype(BF16), upper) + carry
        ranks.append(jnp.sum(before * hit, axis=0, keepdims=True))
        carry = carry + jnp.sum(hit, axis=1, keepdims=True)
    rank = jnp.concatenate(ranks, axis=1).astype(I32)
    x, y, z = dev // n_own, (dev // (2 * N)) % N, (dev // 2) % N
    spot = (x + y + z) % N * G + x * (2 * N) + y * 2 + dev % 2
    code0 = jnp.where(rank < 8, spot * 8 + rank, -1)
    code1 = jnp.where(rank >= 8, spot * 8 + rank - 8, -1)
    code2 = jnp.where(rank >= 8, spot * 4 + rank - 8, -1)

    r16 = iota((16, rows), 0)
    slots = one_hot((r16 % 4 == slot) & (r16 < 12))
    half = jnp.concatenate([mel_ref[...], slots], axis=0)
    mel2[...] = jnp.concatenate([half, half], axis=0).T

    pl.semaphore_wait(barrier, devices - 1)

    tile = G * 8
    low = iota((tile, 128), 1) < 64
    lines = jnp.concatenate([iota((tile, 128), 0).astype(F32).astype(BF16)] * (rows // 128), axis=1)

    def spread(code, g):
        code = jnp.broadcast_to((code - g * tile).astype(F32), (16, rows)).astype(BF16)
        return jnp.concatenate([code] * (tile // 16), axis=0)

    one, zero = jnp.ones((), BF16), jnp.zeros((), BF16)

    def send(slot_, to):
        pltpu.make_async_remote_copy(
            src_ref=snd.at[slot_],
            dst_ref=rcv.at[place],
            send_sem=ssem,
            recv_sem=rsem.at[mine_k],
            device_id=to,
            device_id_type=MESH,
        ).start()

    def pack(j, c):
        g = (mine_k + j) % groups
        picks = jnp.concatenate(
            [
                jnp.where(lines == spread(code0, g), one, zero),
                jnp.where(lines == spread(code1, g), one, zero),
            ],
            axis=0,
        )
        both = mm(picks, mel2[...])
        packed = jnp.where(low, both[:tile], both[tile:]).astype(BF16)
        snd[pl.ds(g * G, G)] = packed.reshape(G, 8, 128)

        each_peer(j, g, send)
        return c

    lax.fori_loop(0, groups, pack, 0)
    rcv[pl.ds(place, 1)] = snd[pl.ds(place, 1)]

    r4 = iota((16, width), 0)
    states = mm(conv_ref[...], w_state_ref[...])
    tiled = jnp.zeros((16, width), F32)
    for s in range(sess):
        tiled = jnp.where(r4 % 4 == s, states[s : s + 1, :], tiled)
    hi = tiled.astype(BF16).astype(F32)
    mid = (tiled - hi).astype(BF16).astype(F32)
    lo = tiled - hi - mid
    terms = jnp.where(r4 < 4, hi, jnp.where(r4 < 8, mid, jnp.where(r4 < 12, lo, 0.0)))
    lanes4 = jnp.where((iota((16, width), 1) // 64 == r4) & (r4 < 4), 1.0, 0.0)
    lengths = [lens_ref[me * sess + s] for s in range(sess)]
    wx[...] = jnp.zeros_like(wx)
    wx[0:mel, 0:width] = w_in_ref[...]
    wx[mel : mel + 16, :] = jnp.concatenate([terms, lanes4], axis=1).astype(BF16)
    lane = iota((1, width), 1)
    past = jnp.zeros((1, width), F32)
    for s in range(sess):
        past = jnp.where(lane == 64 * s, (window - lengths[s]).astype(F32), past)

    low_w = iota((width, 128), 1) < 64
    for pair in range(HEADS // 2):
        w = w_qkv_ref[:, pair * 128 : pair * 128 + 128].astype(F32) * 0.125
        turned = pltpu.roll(w, 64, 1)
        wq[:, pair * 256 : pair * 256 + 128] = jnp.where(low_w, w, turned).astype(BF16)
        wq[:, pair * 256 + 128 : pair * 256 + 256] = jnp.where(low_w, turned, w).astype(BF16)
    wq[:, 2 * width :] = w_qkv_ref[:, width:]

    kv_copy.wait()
    low_p = iota((window, 128), 1) < 64
    row_p = iota((window, 128), 0)

    def turn(a, by):
        return jnp.concatenate([a[window - by :], a[: window - by]], axis=0) if by else a

    for sp in range(2):
        there = slice(sp * 128, sp * 128 + 128)
        in_one = row_p < lengths[2 * sp]
        in_two = row_p < lengths[2 * sp + 1]
        for pair in range(HEADS // 2):
            cols = slice(pair * 128, pair * 128 + 128)
            for which in range(2):
                one_ = kvb[2 * sp, which, :, cols].astype(F32)
                two_ = kvb[2 * sp + 1, which, :, cols].astype(F32)
                if which == 0:
                    one_ = jnp.where(in_one, one_, one_[0:1, :])
                    two_ = jnp.where(in_two, two_, two_[0:1, :])
                else:
                    one_ = jnp.where(in_one, one_, 0.0)
                    two_ = jnp.where(in_two, two_, 0.0)
                one_ = turn(one_, 64 * (2 * sp))
                two_ = turn(two_, 64 * (2 * sp + 1))
                even = jnp.where(low_p, one_, pltpu.roll(two_, 64, 1)).astype(BF16)
                odd = jnp.where(low_p, pltpu.roll(one_, 64, 1), two_).astype(BF16)
                if which == 0:
                    kt[2 * pair, there, :] = even.T
                    kt[2 * pair + 1, there, :] = odd.T
                else:
                    vc[2 * pair, :, there] = even
                    vc[2 * pair + 1, :, there] = odd

    diag = iota((128, 128), 0) == iota((128, 128), 1)
    for b in range(rows // 128):
        here = slice(b * 128, b * 128 + 128)
        c0 = jnp.sum(jnp.where(diag, code0[:, here].astype(F32), 0.0), axis=1, keepdims=True)
        c2 = jnp.sum(jnp.where(diag, code2[:, here].astype(F32), 0.0), axis=1, keepdims=True)
        across = iota((128, 256), 1).astype(F32).astype(BF16)
        for t in range(devices * 8 // 256):
            near = jnp.broadcast_to(c0 - t * 256, (128, 256)).astype(BF16)
            um[here, t * 256 : t * 256 + 256] = jnp.where(across == near, one, zero)
        for t in range(devices * 4 // 256):
            near = jnp.broadcast_to(c2 - t * 256, (128, 256)).astype(BF16)
            ue[here, t * 256 : t * 256 + 256] = jnp.where(across == near, one, zero)

    total = 12 * G
    sums[...] = jnp.zeros_like(sums)
    counts[...] = jnp.zeros_like(counts)
    pick = one_hot(
        (iota((4 * G, 8 * G), 0) // 4 == iota((4 * G, 8 * G), 1) // 8)
        & (iota((4 * G, 8 * G), 0) % 4 == iota((4 * G, 8 * G), 1) % 8)
    )
    slot_lane = one_hot((iota((8, 128), 1) == iota((8, 128), 0) + mel) & (iota((8, 128), 0) < sess))
    low_r = iota((total, 128), 1) < 64
    sub = iota((G // 2, 8, 128), 1) < 4

    def score(j, c):
        g = (mine_k + groups - j) % groups

        @pl.when(j == 0)
        def _():
            part = rcv.at[pl.ds(g * G, G - 1)]
            pltpu.make_async_copy(part, part, rsem.at[g]).wait()

        @pl.when(j > 0)
        def _():
            part = rcv.at[pl.ds(g * G, G)]
            pltpu.make_async_copy(part, part, rsem.at[g]).wait()

        a = rcv[pl.ds(g * G, G)].reshape(8 * G, 128)
        x = pltpu.roll(mm(pick, a), 64, 1).astype(BF16)
        both = jnp.concatenate([a, x], axis=0)
        f = mm(both, wx[...])
        pre = f[:, :width]
        in_lanes = f[:, width : 2 * width]
        mask4 = in_lanes.astype(BF16)
        spare = in_lanes * past
        hidden = (pre * jax.nn.sigmoid(pre)).astype(BF16)
        qkv = mm(hidden, wq[...])
        outs = []
        for pair in range(HEADS // 2):
            kcol = 2 * width + pair * 128
            k = qkv[:, kcol : kcol + 128]
            v = qkv[:, kcol + width : kcol + width + 128]
            mixed, tops, totals, qs = [], [], [], []
            for h in range(2):
                at = pair * 256 + h * 128
                qs.append(qkv[:, at : at + 128])
                q = qs[h].astype(BF16)
                wide = jnp.concatenate([q, q], axis=1) * mask4
                s = mm(wide, kt[2 * pair + h])
                top = jnp.max(s, axis=1, keepdims=True)
                e = jnp.exp(s - top)
                part = (e[:, :128] + e[:, 128:256]) + (e[:, 256:384] + e[:, 384:])
                part = part - spare[:, :128] * e[:, :128] - spare[:, 128:] * e[:, 128:256]
                totals.append(jnp.sum(part, axis=1, keepdims=True))
                tops.append(top)
                o = mm(e.astype(BF16), vc[2 * pair + h])
                mixed.append(o[:, :128] * in_lanes[:, :128] + o[:, 128:] * in_lanes[:, 128:])
            mix = jnp.where(low_r, mixed[0], mixed[1]) + pltpu.roll(
                jnp.where(low_r, mixed[1], mixed[0]), 64, 1
            )
            top = jnp.where(low_r, tops[0], tops[1])
            tot = jnp.where(low_r, totals[0], totals[1])
            prod = jnp.where(low_r, qs[0], qs[1]) * k
            own0 = jnp.sum(jnp.where(low_r, prod, 0.0), axis=1, keepdims=True)
            own1 = jnp.sum(jnp.where(low_r, 0.0, prod), axis=1, keepdims=True)
            mine = jnp.where(low_r, own0, own1)
            peak = jnp.maximum(top, mine)
            ea = jnp.exp(top - peak)
            eb = jnp.exp(mine - peak)
            outs.append(((ea * mix + eb * v) / (ea * tot + eb)).astype(BF16))
        attn = jnp.concatenate(outs, axis=1)
        scored = (hidden.astype(F32) + mm(attn, w_out_ref[...])).astype(BF16)
        wide = scored.astype(F32)
        first = pl.ds(g * G, G)
        rsnd[first, 0:8, :] = scored[: 8 * G, :128].reshape(G, 8, 128)
        rsnd[first, 8:16, :] = scored[: 8 * G, 128:].reshape(G, 8, 128)
        left = wide[8 * G :, :128].reshape(G // 2, 8, 128)
        right = wide[8 * G :, 128:].reshape(G // 2, 8, 128)
        ones = jnp.where(sub, left, pltpu.roll(right, 4, 1))
        twos = jnp.where(sub, pltpu.roll(left, 4, 1), right)
        rsnd[first, 16:24, :] = jnp.stack([ones, twos], axis=1).reshape(G, 8, 128).astype(BF16)

        def back(slot_, to):
            pltpu.make_async_remote_copy(
                src_ref=rsnd.at[slot_],
                dst_ref=ret.at[place],
                send_sem=bsem,
                recv_sem=csem.at[mine_k],
                device_id=to,
                device_id_type=MESH,
            ).start()

        each_peer(j, g, back)
        marks = lax.dot_general(
            slot_lane, both, (((1,), (1,)), ((), ())), preferred_element_type=F32
        )
        sums[...] += mm(marks.astype(BF16), scored)
        counts[...] += jnp.sum(marks, axis=1, keepdims=True)
        return c

    lax.fori_loop(0, groups, score, 0)
    ret[pl.ds(place, 1)] = rsnd[pl.ds(place, 1)]

    n = counts[0:sess, 0:1]
    mean = sums[0:sess, :] / jnp.maximum(n, 1.0)
    updated = jnp.where(n > 0, mean, conv_ref[...].astype(F32)).astype(BF16).astype(F32)
    upd_out[...] = jnp.zeros_like(upd_out)
    upd_out[0:sess, :] = updated
    push = pltpu.make_async_remote_copy(
        src_ref=upd_out,
        dst_ref=upd_in,
        send_sem=usem.at[0],
        recv_sem=usem.at[1],
        device_id=(ing, lax.rem(own + 1, n_own)),
        device_id_type=MESH,
    )
    push.start()
    sub = iota((G // 2, 8, 128), 1) < 4

    def unpack(j, c):
        k = (mine_k + j) % groups

        @pl.when(j == 0)
        def _():
            part = ret.at[pl.ds(k * G, G - 1)]
            pltpu.make_async_copy(part, part, csem.at[k]).wait()

        @pl.when(j > 0)
        def _():
            part = ret.at[pl.ds(k * G, G)]
            pltpu.make_async_copy(part, part, csem.at[k]).wait()

        here = pl.ds(k * G, G)
        main = jnp.concatenate(
            [
                ret[here, 0:8, :].reshape(G * 8, 128),
                ret[here, 8:16, :].reshape(G * 8, 128),
            ],
            axis=1,
        )
        extra = ret[here, 16:24, :].astype(F32).reshape(G // 2, 2, 8, 128)
        ones, twos = extra[:, 0], extra[:, 1]
        left = jnp.where(sub, ones, pltpu.roll(twos, 4, 1)).reshape(G * 4, 128)
        right = jnp.where(sub, pltpu.roll(ones, 4, 1), twos).reshape(G * 4, 128)
        extra = jnp.concatenate([left, right], axis=1).astype(BF16)
        mains = um[:, pl.ds(pl.multiple_of(k * (G * 8), 256), G * 8)]
        extras = ue[:, pl.ds(pl.multiple_of(k * (G * 4), 128), G * 4)]
        more = mm(mains, main) + mm(extras, extra)

        @pl.when(j == 0)
        def _():
            acc[...] = more

        @pl.when((j > 0) & (j < groups - 1))
        def _():
            acc[...] += more

        @pl.when(j == groups - 1)
        def _():
            out_ref[...] = (acc[...] + more).astype(BF16)

        return c

    lax.fori_loop(0, groups, unpack, 0)
    other = snd.at[pl.ds(0, devices - 1)]
    pltpu.make_async_copy(other, other, ssem).wait()
    other = rsnd.at[pl.ds(0, devices - 1)]
    pltpu.make_async_copy(other, other, bsem).wait()
    push.wait()
    r8 = iota((8, width), 0)
    prev = ing * n_own + lax.rem(own + n_own - 1, n_own)
    keep = (r8 < sess) & (r8 < sess - mig_ref[me])
    live = (r8 >= sess) & (r8 - sess >= MIG - mig_ref[prev])
    table = jnp.where(
        keep, upd_out[...], jnp.where(live, pltpu.roll(upd_in[...], MIG, 0), 0.0)
    ).astype(BF16)
    new_ref[...] = table[0 : sess + MIG, :]


def body(
    frame_mel,
    row_device,
    row_slot,
    window_length,
    migrate_count,
    conv_state,
    kv_cache,
    w_in,
    w_state,
    w_qkv,
    w_out,
):
    n_ing = lax.axis_size("ingest")
    n_own = lax.axis_size("owner")
    devices = n_ing * n_own
    rows, mel = frame_mel.shape
    sess, _, window, width = kv_cache.shape
    G = n_own
    groups = devices // G
    vmem = pl.BlockSpec(memory_space=pltpu.VMEM)
    smem = pl.BlockSpec(memory_space=pltpu.SMEM)
    return pl.pallas_call(
        functools.partial(kernel, n_ing, n_own, G),
        out_shape=(
            jax.ShapeDtypeStruct((rows, width), BF16),
            jax.ShapeDtypeStruct((sess + MIG, width), BF16),
        ),
        in_specs=[
            vmem,
            vmem,
            smem,
            smem,
            vmem,
            vmem,
            pl.BlockSpec(memory_space=pl.ANY),
            vmem,
            vmem,
            vmem,
            vmem,
        ],
        out_specs=(vmem, vmem),
        scratch_shapes=[
            pltpu.VMEM((devices, 8, 128), BF16),
            pltpu.VMEM((devices, 8, 128), BF16),
            pltpu.VMEM((devices, 24, 128), BF16),
            pltpu.VMEM((devices, 24, 128), BF16),
            pltpu.VMEM(kv_cache.shape, BF16),
            pltpu.VMEM((HEADS, width, window), BF16),
            pltpu.VMEM((HEADS, window, width), BF16),
            pltpu.VMEM((rows, 128), BF16),
            pltpu.VMEM((rows, devices * 8), BF16),
            pltpu.VMEM((rows, devices * 4), BF16),
            pltpu.VMEM((128, 2 * width), BF16),
            pltpu.VMEM((width, 4 * width), BF16),
            pltpu.VMEM((8, width), F32),
            pltpu.VMEM((8, 128), F32),
            pltpu.VMEM((8, width), F32),
            pltpu.VMEM((8, width), F32),
            pltpu.VMEM((rows, width), F32),
            pltpu.SemaphoreType.DMA,
            pltpu.SemaphoreType.DMA,
            pltpu.SemaphoreType.DMA((groups,)),
            pltpu.SemaphoreType.DMA,
            pltpu.SemaphoreType.DMA((groups,)),
            pltpu.SemaphoreType.DMA((2,)),
        ],
        compiler_params=pltpu.CompilerParams(
            collective_id=0, has_side_effects=True, vmem_limit_bytes=56 << 20
        ),
        name="scorer",
    )(
        row_device.reshape(1, rows),
        row_slot.reshape(1, rows),
        window_length,
        migrate_count,
        conv_state,
        frame_mel.T,
        kv_cache,
        w_in,
        w_state,
        w_qkv,
        w_out,
    )


def solution(mesh):
    placed = (
        P(("ingest", "owner"), None),
        P(("ingest", "owner"), None),
        P(("ingest", "owner")),
        P(),
        P(),
        P(("ingest", "owner"), None),
        P(("ingest", "owner"), None, None, None),
        P(),
        P(),
        P(),
        P(),
    )
    return jax.shard_map(
        body,
        mesh=mesh,
        in_specs=placed,
        out_specs=(P(("ingest", "owner"), None), P(("ingest", "owner"), None)),
        check_vma=False,
    )
```

```python
import functools

import jax
import jax.numpy as jnp
from jax import lax
from jax.experimental import pallas as pl
from jax.experimental.pallas import tpu as pltpu
from jax.sharding import PartitionSpec as P

HEADS = 4
MIG = 2
LOG2E = 1.4426950408889634
MESH = pl.DeviceIdType.MESH
F32 = jnp.float32
BF16 = jnp.bfloat16
I32 = jnp.int32


def iota(shape, dim):
    return lax.broadcasted_iota(I32, shape, dim)


def one_hot(mask):
    return jnp.where(mask, 1.0, 0.0).astype(BF16)


def mm(a, b):
    return jnp.dot(a, b, preferred_element_type=F32)


def kernel(
    n_ing,
    n_own,
    G,
    dev_hbm,
    slot_hbm,
    lens_hbm,
    mig_hbm,
    conv_hbm,
    mel_hbm,
    kv_ref,
    w_in_hbm,
    w_state_hbm,
    w_qkv_hbm,
    w_out_hbm,
    out_ref,
    new_ref,
    dev_ref,
    slot_ref,
    lens_ref,
    mig_ref,
    conv_ref,
    mel_ref,
    w_in_ref,
    w_state_ref,
    w_qkv_ref,
    w_out_ref,
    snd,
    rcv,
    rsnd,
    ret,
    kvb,
    kt,
    vc,
    mel2,
    um,
    ue,
    wx,
    wq,
    sums,
    counts,
    upd_out,
    upd_in,
    acc,
    marks,
    lanes,
    hid,
    qkvs,
    kv_sem,
    ssem,
    rsem,
    bsem,
    csem,
    usem,
    in_sem,
):
    devices = n_ing * n_own
    groups = devices // G
    rows = mel_ref.shape[1]
    mel = mel_ref.shape[0]
    sess, width = conv_ref.shape
    window = kv_ref.shape[2]
    ing = lax.axis_index("ingest")
    own = lax.axis_index("owner")
    me = ing * n_own + own

    N = n_ing
    rem = lax.rem
    yy, zz, core = lax.div(own, 2 * N), rem(lax.div(own, 2), N), rem(own, 2)
    mine_k = rem(ing + yy + zz, N)
    place = mine_k * G + ing * (2 * N) + yy * 2 + core

    def peer(k, dx, dy, dc):
        x, y, c = rem(ing + dx, N), rem(yy + dy, N), rem(core + dc, 2)
        z = rem(k + 2 * N - x - y, N)
        return k * G + x * (2 * N) + y * 2 + c, (x, y * (2 * N) + z * 2 + c)

    def each_peer(j, k, start):
        def step(dx, c):
            for dy in range(N):
                for dc in range(2):
                    if dy + dc > 0:
                        start(*peer(k, dx, dy, dc))
            return c

        lax.fori_loop(0, N, step, 0)
        for dx in range(1, N):
            start(*peer(k, dx, 0, 0))
        if j > 0:
            start(*peer(k, 0, 0, 0))

    pairs = [
        (dev_hbm, dev_ref),
        (slot_hbm, slot_ref),
        (mel_hbm, mel_ref),
        (lens_hbm, lens_ref),
        (conv_hbm, conv_ref),
        (w_state_hbm, w_state_ref),
        (w_in_hbm, w_in_ref),
        (w_qkv_hbm, w_qkv_ref),
        (w_out_hbm, w_out_ref),
        (mig_hbm, mig_ref),
    ]
    loads = [pltpu.make_async_copy(a, b, in_sem.at[i]) for i, (a, b) in enumerate(pairs)]
    for load in loads:
        load.start()
    kv_copy = pltpu.make_async_copy(kv_ref, kvb, kv_sem)
    kv_copy.start()

    barrier = pltpu.get_barrier_semaphore()

    def greet(i, c):
        for a in range(n_ing):
            x = lax.rem(ing + a, n_ing)
            y = lax.rem(own + i, n_own)
            pl.semaphore_signal(barrier, inc=1, device_id=(x, y), device_id_type=MESH)
        return c

    lax.fori_loop(1, n_own, greet, 0, unroll=4)
    for a in range(1, n_ing):
        x = lax.rem(ing + a, n_ing)
        pl.semaphore_signal(barrier, inc=1, device_id=(x, own), device_id_type=MESH)

    for load in loads[:3]:
        load.wait()
    dev = dev_ref[...]
    slot = slot_ref[...]
    step = 256
    upper = one_hot(iota((step, step), 0) < iota((step, step), 1))
    lane_dev = iota((devices, step), 0)
    carry = jnp.zeros((devices, 1), F32)
    ranks = []
    for b in range(rows // step):
        hit = jnp.where(lane_dev == dev[:, b * step : (b + 1) * step], 1.0, 0.0)
        before = mm(hit.astype(BF16), upper) + carry
        ranks.append(jnp.sum(before * hit, axis=0, keepdims=True))
        carry = carry + jnp.sum(hit, axis=1, keepdims=True)
    rank = jnp.concatenate(ranks, axis=1).astype(I32)
    x, y, z = dev // n_own, (dev // (2 * N)) % N, (dev // 2) % N
    spot = (x + y + z) % N * G + x * (2 * N) + y * 2 + dev % 2
    code0 = jnp.where(rank < 8, spot * 8 + rank, -1)
    code1 = jnp.where(rank >= 8, spot * 8 + rank - 8, -1)
    code2 = jnp.where(rank >= 8, spot * 4 + rank - 8, -1)

    r16 = iota((16, rows), 0)
    slots = one_hot((r16 % 4 == slot) & (r16 < 12))
    half = jnp.concatenate([mel_ref[...], slots], axis=0)
    mel2[...] = jnp.concatenate([half, half], axis=0).T

    tile = G * 8
    low = iota((tile, 128), 1) < 64
    lines = jnp.concatenate([iota((tile, 128), 0).astype(F32).astype(BF16)] * (rows // 128), axis=1)

    def spread(code, g):
        code = jnp.broadcast_to((code - g * tile).astype(F32), (16, rows)).astype(BF16)
        return jnp.concatenate([code] * (tile // 16), axis=0)

    one, zero = jnp.ones((), BF16), jnp.zeros((), BF16)

    def send(slot_, to):
        pltpu.make_async_remote_copy(
            src_ref=snd.at[slot_],
            dst_ref=rcv.at[place],
            send_sem=ssem,
            recv_sem=rsem.at[mine_k],
            device_id=to,
            device_id_type=MESH,
        ).start()

    for g in range(groups):
        picks = jnp.concatenate(
            [
                jnp.where(lines == spread(code0, g), one, zero),
                jnp.where(lines == spread(code1, g), one, zero),
            ],
            axis=0,
        )
        both = mm(picks, mel2[...])
        packed = jnp.where(low, both[:tile], both[tile:]).astype(BF16)
        snd[g * G : g * G + G] = packed.reshape(G, 8, 128)

    pl.semaphore_wait(barrier, devices - 1)
    for j in range(groups):
        each_peer(j, rem(mine_k + j, groups), send)
    rcv[pl.ds(place, 1)] = snd[pl.ds(place, 1)]

    for load in loads[3:]:
        load.wait()
    r4 = iota((16, width), 0)
    states = mm(conv_ref[...], w_state_ref[...])
    tiled = jnp.zeros((16, width), F32)
    for s in range(sess):
        tiled = jnp.where(r4 % 4 == s, states[s : s + 1, :], tiled)
    hi = tiled.astype(BF16).astype(F32)
    mid = (tiled - hi).astype(BF16).astype(F32)
    lo = tiled - hi - mid
    terms = jnp.where(r4 < 4, hi, jnp.where(r4 < 8, mid, jnp.where(r4 < 12, lo, 0.0)))
    lanes4 = jnp.where((iota((16, width), 1) // 64 == r4) & (r4 < 4), 1.0, 0.0)
    lengths = [lens_ref[me * sess + s] for s in range(sess)]
    wx[...] = jnp.zeros_like(wx)
    wx[0:mel, 0:width] = w_in_ref[...]
    wx[mel : mel + 16, :] = jnp.concatenate([terms, lanes4], axis=1).astype(BF16)
    lane = iota((1, width), 1)
    past = jnp.zeros((1, width), F32)
    for s in range(sess):
        past = jnp.where(lane == 64 * s, (window - lengths[s]).astype(F32), past)

    low_w = iota((width, 128), 1) < 64
    for pair in range(HEADS // 2):
        w = w_qkv_ref[:, pair * 128 : pair * 128 + 128].astype(F32) * 0.125
        turned = pltpu.roll(w, 64, 1)
        wq[:, pair * 256 : pair * 256 + 128] = jnp.where(low_w, w, turned).astype(BF16)
        wq[:, pair * 256 + 128 : pair * 256 + 256] = jnp.where(low_w, turned, w).astype(BF16)
    wq[:, 2 * width :] = w_qkv_ref[:, width:]

    kv_copy.wait()
    low_p = iota((window, 128), 1) < 64
    row_p = iota((window, 128), 0)

    def turn(a, by):
        return jnp.concatenate([a[window - by :], a[: window - by]], axis=0) if by else a

    for sp in range(2):
        there = slice(sp * 128, sp * 128 + 128)
        in_one = row_p < lengths[2 * sp]
        in_two = row_p < lengths[2 * sp + 1]
        for pair in range(HEADS // 2):
            cols = slice(pair * 128, pair * 128 + 128)
            for which in range(2):
                one_ = kvb[2 * sp, which, :, cols].astype(F32)
                two_ = kvb[2 * sp + 1, which, :, cols].astype(F32)
                if which == 0:
                    one_ = jnp.where(in_one, one_, one_[0:1, :])
                    two_ = jnp.where(in_two, two_, two_[0:1, :])
                else:
                    one_ = jnp.where(in_one, one_, 0.0)
                    two_ = jnp.where(in_two, two_, 0.0)
                one_ = turn(one_, 64 * (2 * sp))
                two_ = turn(two_, 64 * (2 * sp + 1))
                even = jnp.where(low_p, one_, pltpu.roll(two_, 64, 1)).astype(BF16)
                odd = jnp.where(low_p, pltpu.roll(one_, 64, 1), two_).astype(BF16)
                if which == 0:
                    kt[2 * pair, there, :] = even.T
                    kt[2 * pair + 1, there, :] = odd.T
                else:
                    vc[2 * pair, :, there] = even
                    vc[2 * pair + 1, :, there] = odd

    total = 12 * G
    sums[...] = jnp.zeros_like(sums)
    counts[...] = jnp.zeros_like(counts)
    pick = one_hot(
        (iota((4 * G, 8 * G), 0) // 4 == iota((4 * G, 8 * G), 1) // 8)
        & (iota((4 * G, 8 * G), 0) % 4 == iota((4 * G, 8 * G), 1) % 8)
    )
    slot_lane = one_hot((iota((8, 128), 1) == iota((8, 128), 0) + mel) & (iota((8, 128), 0) < sess))
    low_r = iota((total, 128), 1) < 64
    sub = iota((G // 2, 8, 128), 1) < 4

    def front(j):
        g = rem(mine_k + groups - j, groups)
        part = rcv.at[pl.ds(g * G, G if j else G - 1)]
        pltpu.make_async_copy(part, part, rsem.at[g]).wait()
        a = rcv[pl.ds(g * G, G)].reshape(8 * G, 128)
        x = pltpu.roll(mm(pick, a), 64, 1).astype(BF16)
        both = jnp.concatenate([a, x], axis=0)
        f = mm(both, wx[...])
        pre = f[:, :width]
        hidden = (pre * jax.nn.sigmoid(pre)).astype(BF16)
        marks[j % 2] = both
        lanes[j % 2] = f[:, width:]
        hid[j % 2] = hidden
        qkv = mm(hidden, wq[...])
        qkvs[j % 2, :, : 2 * width] = qkv[:, : 2 * width] * LOG2E
        qkvs[j % 2, :, 2 * width :] = qkv[:, 2 * width :]

    def heads(j):
        g = rem(mine_k + groups - j, groups)
        qkv = qkvs.at[j % 2]
        in_lanes = lanes[j % 2]
        mask4 = in_lanes.astype(BF16)
        kept = 1.0 - in_lanes * past
        hidden = hid[j % 2]
        outs = []
        for pair in range(HEADS // 2):
            kcol = 2 * width + pair * 128
            k = qkv[:, kcol : kcol + 128]
            v = qkv[:, kcol + width : kcol + width + 128]
            mixed, tops, totals, qs = [], [], [], []
            for h in range(2):
                at = pair * 256 + h * 128
                qs.append(qkv[:, at : at + 128])
                q = qs[h].astype(BF16)
                wide = jnp.concatenate([q, q], axis=1) * mask4
                s = mm(wide, kt[2 * pair + h])
                top = jnp.max(s, axis=1, keepdims=True)
                e = jnp.exp2(s - top)
                part = (e[:, :128] * kept[:, :128] + e[:, 128:256] * kept[:, 128:]) + (
                    e[:, 256:384] + e[:, 384:]
                )
                totals.append(jnp.sum(part, axis=1, keepdims=True))
                tops.append(top)
                o = mm(e.astype(BF16), vc[2 * pair + h])
                mixed.append(o[:, :128] * in_lanes[:, :128] + o[:, 128:] * in_lanes[:, 128:])
            mix = jnp.where(low_r, mixed[0], mixed[1]) + pltpu.roll(
                jnp.where(low_r, mixed[1], mixed[0]), 64, 1
            )
            top = jnp.where(low_r, tops[0], tops[1])
            tot = jnp.where(low_r, totals[0], totals[1])
            prod = jnp.where(low_r, qs[0], qs[1]) * k
            own0 = jnp.sum(jnp.where(low_r, prod, 0.0), axis=1, keepdims=True)
            own1 = jnp.sum(jnp.where(low_r, 0.0, prod), axis=1, keepdims=True)
            mine = jnp.where(low_r, own0, own1)
            peak = jnp.maximum(top, mine)
            ea = jnp.exp2(top - peak)
            eb = jnp.exp2(mine - peak)
            outs.append(((ea * mix + eb * v) / (ea * tot + eb)).astype(BF16))
        attn = jnp.concatenate(outs, axis=1)
        scored = (hidden.astype(F32) + mm(attn, w_out_ref[...])).astype(BF16)
        wide = scored.astype(F32)
        first = pl.ds(g * G, G)
        rsnd[first, 0:8, :] = scored[: 8 * G, :128].reshape(G, 8, 128)
        rsnd[first, 8:16, :] = scored[: 8 * G, 128:].reshape(G, 8, 128)
        left = wide[8 * G :, :128].reshape(G // 2, 8, 128)
        right = wide[8 * G :, 128:].reshape(G // 2, 8, 128)
        ones = jnp.where(sub, left, pltpu.roll(right, 4, 1))
        twos = jnp.where(sub, pltpu.roll(left, 4, 1), right)
        rsnd[first, 16:24, :] = jnp.stack([ones, twos], axis=1).reshape(G, 8, 128).astype(BF16)

        def back(slot_, to):
            pltpu.make_async_remote_copy(
                src_ref=rsnd.at[slot_],
                dst_ref=ret.at[place],
                send_sem=bsem,
                recv_sem=csem.at[mine_k],
                device_id=to,
                device_id_type=MESH,
            ).start()

        each_peer(j, g, back)
        hits = lax.dot_general(
            slot_lane, marks[j % 2], (((1,), (1,)), ((), ())), preferred_element_type=F32
        )
        sums[...] += mm(hits.astype(BF16), scored)
        counts[...] += jnp.sum(hits, axis=1, keepdims=True)

    front(0)
    for j in range(groups):
        if j + 1 < groups:
            front(j + 1)
        heads(j)
    ret[pl.ds(place, 1)] = rsnd[pl.ds(place, 1)]

    diag = iota((128, 128), 0) == iota((128, 128), 1)
    for b in range(rows // 128):
        here = slice(b * 128, b * 128 + 128)
        c0 = jnp.sum(jnp.where(diag, code0[:, here].astype(F32), 0.0), axis=1, keepdims=True)
        c2 = jnp.sum(jnp.where(diag, code2[:, here].astype(F32), 0.0), axis=1, keepdims=True)
        across = iota((128, 256), 1).astype(F32).astype(BF16)
        for t in range(devices * 8 // 256):
            near = jnp.broadcast_to(c0 - t * 256, (128, 256)).astype(BF16)
            um[here, t * 256 : t * 256 + 256] = jnp.where(across == near, one, zero)
        for t in range(devices * 4 // 256):
            near = jnp.broadcast_to(c2 - t * 256, (128, 256)).astype(BF16)
            ue[here, t * 256 : t * 256 + 256] = jnp.where(across == near, one, zero)

    n = counts[0:sess, 0:1]
    mean = sums[0:sess, :] / jnp.maximum(n, 1.0)
    updated = jnp.where(n > 0, mean, conv_ref[...].astype(F32)).astype(BF16).astype(F32)
    upd_out[...] = jnp.zeros_like(upd_out)
    upd_out[0:sess, :] = updated
    push = pltpu.make_async_remote_copy(
        src_ref=upd_out,
        dst_ref=upd_in,
        send_sem=usem.at[0],
        recv_sem=usem.at[1],
        device_id=(ing, lax.rem(own + 1, n_own)),
        device_id_type=MESH,
    )
    push.start()
    sub = iota((G // 2, 8, 128), 1) < 4

    def unpack(j, c):
        k = (mine_k + j) % groups

        @pl.when(j == 0)
        def _():
            part = ret.at[pl.ds(k * G, G - 1)]
            pltpu.make_async_copy(part, part, csem.at[k]).wait()

        @pl.when(j > 0)
        def _():
            part = ret.at[pl.ds(k * G, G)]
            pltpu.make_async_copy(part, part, csem.at[k]).wait()

        here = pl.ds(k * G, G)
        main = jnp.concatenate(
            [
                ret[here, 0:8, :].reshape(G * 8, 128),
                ret[here, 8:16, :].reshape(G * 8, 128),
            ],
            axis=1,
        )
        extra = ret[here, 16:24, :].astype(F32).reshape(G // 2, 2, 8, 128)
        ones, twos = extra[:, 0], extra[:, 1]
        left = jnp.where(sub, ones, pltpu.roll(twos, 4, 1)).reshape(G * 4, 128)
        right = jnp.where(sub, pltpu.roll(ones, 4, 1), twos).reshape(G * 4, 128)
        extra = jnp.concatenate([left, right], axis=1).astype(BF16)
        mains = um[:, pl.ds(pl.multiple_of(k * (G * 8), 256), G * 8)]
        extras = ue[:, pl.ds(pl.multiple_of(k * (G * 4), 128), G * 4)]
        more = mm(mains, main) + mm(extras, extra)

        @pl.when(j == 0)
        def _():
            acc[...] = more

        @pl.when((j > 0) & (j < groups - 1))
        def _():
            acc[...] += more

        @pl.when(j == groups - 1)
        def _():
            out_ref[...] = (acc[...] + more).astype(BF16)

        return c

    lax.fori_loop(0, groups, unpack, 0)
    other = snd.at[pl.ds(0, devices - 1)]
    pltpu.make_async_copy(other, other, ssem).wait()
    other = rsnd.at[pl.ds(0, devices - 1)]
    pltpu.make_async_copy(other, other, bsem).wait()
    push.wait()
    r8 = iota((8, width), 0)
    prev = ing * n_own + lax.rem(own + n_own - 1, n_own)
    keep = (r8 < sess) & (r8 < sess - mig_ref[me])
    live = (r8 >= sess) & (r8 - sess >= MIG - mig_ref[prev])
    table = jnp.where(
        keep, upd_out[...], jnp.where(live, pltpu.roll(upd_in[...], MIG, 0), 0.0)
    ).astype(BF16)
    new_ref[...] = table[0 : sess + MIG, :]


def body(
    frame_mel,
    row_device,
    row_slot,
    window_length,
    migrate_count,
    conv_state,
    kv_cache,
    w_in,
    w_state,
    w_qkv,
    w_out,
):
    n_ing = lax.axis_size("ingest")
    n_own = lax.axis_size("owner")
    devices = n_ing * n_own
    rows, mel = frame_mel.shape
    sess, _, window, width = kv_cache.shape
    G = n_own
    groups = devices // G
    vmem = pl.BlockSpec(memory_space=pltpu.VMEM)
    return pl.pallas_call(
        functools.partial(kernel, n_ing, n_own, G),
        out_shape=(
            jax.ShapeDtypeStruct((rows, width), BF16),
            jax.ShapeDtypeStruct((sess + MIG, width), BF16),
        ),
        in_specs=[pl.BlockSpec(memory_space=pltpu.HBM)] * 11,
        out_specs=(vmem, vmem),
        scratch_shapes=[
            pltpu.VMEM((1, rows), I32),
            pltpu.VMEM((1, rows), I32),
            pltpu.SMEM(window_length.shape, I32),
            pltpu.SMEM(migrate_count.shape, I32),
            pltpu.VMEM(conv_state.shape, BF16),
            pltpu.VMEM((mel, rows), BF16),
            pltpu.VMEM(w_in.shape, BF16),
            pltpu.VMEM(w_state.shape, BF16),
            pltpu.VMEM(w_qkv.shape, BF16),
            pltpu.VMEM(w_out.shape, BF16),
            pltpu.VMEM((devices, 8, 128), BF16),
            pltpu.VMEM((devices, 8, 128), BF16),
            pltpu.VMEM((devices, 24, 128), BF16),
            pltpu.VMEM((devices, 24, 128), BF16),
            pltpu.VMEM(kv_cache.shape, BF16),
            pltpu.VMEM((HEADS, width, window), BF16),
            pltpu.VMEM((HEADS, window, width), BF16),
            pltpu.VMEM((rows, 128), BF16),
            pltpu.VMEM((rows, devices * 8), BF16),
            pltpu.VMEM((rows, devices * 4), BF16),
            pltpu.VMEM((128, 2 * width), BF16),
            pltpu.VMEM((width, 4 * width), BF16),
            pltpu.VMEM((8, width), F32),
            pltpu.VMEM((8, 128), F32),
            pltpu.VMEM((8, width), F32),
            pltpu.VMEM((8, width), F32),
            pltpu.VMEM((rows, width), F32),
            pltpu.VMEM((2, 12 * G, 128), BF16),
            pltpu.VMEM((2, 12 * G, width), F32),
            pltpu.VMEM((2, 12 * G, width), BF16),
            pltpu.VMEM((2, 12 * G, 4 * width), F32),
            pltpu.SemaphoreType.DMA,
            pltpu.SemaphoreType.DMA,
            pltpu.SemaphoreType.DMA((groups,)),
            pltpu.SemaphoreType.DMA,
            pltpu.SemaphoreType.DMA((groups,)),
            pltpu.SemaphoreType.DMA((2,)),
            pltpu.SemaphoreType.DMA((10,)),
        ],
        compiler_params=pltpu.CompilerParams(
            collective_id=0, has_side_effects=True, vmem_limit_bytes=40 << 20
        ),
        name="scorer",
    )(
        *(
            pltpu.with_memory_space_constraint(a, pltpu.HBM)
            for a in (
                row_device.reshape(1, rows),
                row_slot.reshape(1, rows),
                window_length,
                migrate_count,
                conv_state,
                frame_mel.T,
                kv_cache,
                w_in,
                w_state,
                w_qkv,
                w_out,
            )
        )
    )


def solution(mesh):
    placed = (
        P(("ingest", "owner"), None),
        P(("ingest", "owner"), None),
        P(("ingest", "owner")),
        P(),
        P(),
        P(("ingest", "owner"), None),
        P(("ingest", "owner"), None, None, None),
        P(),
        P(),
        P(),
        P(),
    )
    return jax.shard_map(
        body,
        mesh=mesh,
        in_specs=placed,
        out_specs=(P(("ingest", "owner"), None), P(("ingest", "owner"), None)),
        check_vma=False,
    )
```

```python
import functools

import jax
import jax.numpy as jnp
from jax import lax
from jax.experimental import pallas as pl
from jax.experimental.pallas import tpu as pltpu
from jax.sharding import PartitionSpec as P

HEADS = 4
MIG = 2
LOG2E = 1.4426950408889634
MESH = pl.DeviceIdType.MESH
F32 = jnp.float32
BF16 = jnp.bfloat16
I32 = jnp.int32


def iota(shape, dim):
    return lax.broadcasted_iota(I32, shape, dim)


def one_hot(mask):
    return jnp.where(mask, 1.0, 0.0).astype(BF16)


def mm(a, b):
    return jnp.dot(a, b, preferred_element_type=F32)


def kernel(
    n_ing,
    n_own,
    G,
    dev_hbm,
    slot_hbm,
    lens_hbm,
    mig_hbm,
    conv_hbm,
    mel_hbm,
    kv_ref,
    w_in_hbm,
    w_state_hbm,
    w_qkv_hbm,
    w_out_hbm,
    out_ref,
    new_ref,
    dev_ref,
    slot_ref,
    lens_ref,
    mig_ref,
    conv_ref,
    mel_ref,
    w_in_ref,
    w_state_ref,
    w_qkv_ref,
    w_out_ref,
    snd,
    rcv,
    rsnd,
    ret,
    kvb,
    kt,
    vc,
    mel2,
    um,
    ue,
    wx,
    wq,
    sums,
    counts,
    upd_out,
    upd_in,
    acc,
    marks,
    raw,
    expo,
    lanes,
    masks,
    kept,
    hid,
    qkvs,
    kv_sem,
    ssem,
    rsem,
    bsem,
    csem,
    usem,
    in_sem,
):
    devices = n_ing * n_own
    groups = devices // G
    rows = mel_ref.shape[1]
    mel = mel_ref.shape[0]
    sess, width = conv_ref.shape
    window = kv_ref.shape[2]
    ing = lax.axis_index("ingest")
    own = lax.axis_index("owner")
    me = ing * n_own + own

    N = n_ing
    rem = lax.rem
    yy, zz, core = lax.div(own, 2 * N), rem(lax.div(own, 2), N), rem(own, 2)
    mine_k = rem(ing + yy + zz, N)
    place = mine_k * G + ing * (2 * N) + yy * 2 + core

    def peer(k, dx, dy, dc):
        x, y, c = rem(ing + dx, N), rem(yy + dy, N), rem(core + dc, 2)
        z = rem(k + 2 * N - x - y, N)
        return k * G + x * (2 * N) + y * 2 + c, (x, y * (2 * N) + z * 2 + c)

    def each_peer(j, k, start):
        def step(dx, c):
            for dy in range(N):
                for dc in range(2):
                    if dy + dc > 0:
                        start(*peer(k, dx, dy, dc))
            return c

        lax.fori_loop(0, N, step, 0)
        for dx in range(1, N):
            start(*peer(k, dx, 0, 0))
        if j > 0:
            start(*peer(k, 0, 0, 0))

    pairs = [
        (dev_hbm, dev_ref),
        (slot_hbm, slot_ref),
        (mel_hbm, mel_ref),
        (lens_hbm, lens_ref),
        (conv_hbm, conv_ref),
        (w_state_hbm, w_state_ref),
        (w_in_hbm, w_in_ref),
        (w_qkv_hbm, w_qkv_ref),
        (w_out_hbm, w_out_ref),
        (mig_hbm, mig_ref),
    ]
    loads = [pltpu.make_async_copy(a, b, in_sem.at[i]) for i, (a, b) in enumerate(pairs)]
    for load in loads:
        load.start()
    kv_copy = pltpu.make_async_copy(kv_ref, kvb, kv_sem)
    kv_copy.start()

    barrier = pltpu.get_barrier_semaphore()

    def greet(i, c):
        for a in range(n_ing):
            x = lax.rem(ing + a, n_ing)
            y = lax.rem(own + i, n_own)
            pl.semaphore_signal(barrier, inc=1, device_id=(x, y), device_id_type=MESH)
        return c

    lax.fori_loop(1, n_own, greet, 0, unroll=4)
    for a in range(1, n_ing):
        x = lax.rem(ing + a, n_ing)
        pl.semaphore_signal(barrier, inc=1, device_id=(x, own), device_id_type=MESH)

    for load in loads[:3]:
        load.wait()
    dev = dev_ref[...]
    slot = slot_ref[...]
    step = 256
    upper = one_hot(iota((step, step), 0) < iota((step, step), 1))
    lane_dev = iota((devices, step), 0)
    carry = jnp.zeros((devices, 1), F32)
    ranks = []
    for b in range(rows // step):
        hit = jnp.where(lane_dev == dev[:, b * step : (b + 1) * step], 1.0, 0.0)
        before = mm(hit.astype(BF16), upper) + carry
        ranks.append(jnp.sum(before * hit, axis=0, keepdims=True))
        carry = carry + jnp.sum(hit, axis=1, keepdims=True)
    rank = jnp.concatenate(ranks, axis=1).astype(I32)
    x, y, z = dev // n_own, (dev // (2 * N)) % N, (dev // 2) % N
    spot = (x + y + z) % N * G + x * (2 * N) + y * 2 + dev % 2
    code0 = jnp.where(rank < 8, spot * 8 + rank, -1)
    code1 = jnp.where(rank >= 8, spot * 8 + rank - 8, -1)
    code2 = jnp.where(rank >= 8, spot * 4 + rank - 8, -1)

    r16 = iota((16, rows), 0)
    slots = one_hot((r16 % 4 == slot) & (r16 < 12))
    half = jnp.concatenate([mel_ref[...], slots], axis=0)
    mel2[...] = jnp.concatenate([half, half], axis=0).T

    tile = G * 8
    low = iota((tile, 128), 1) < 64
    lines = jnp.concatenate([iota((tile, 128), 0).astype(F32).astype(BF16)] * (rows // 128), axis=1)

    def spread(code, g):
        code = jnp.broadcast_to((code - g * tile).astype(F32), (16, rows)).astype(BF16)
        return jnp.concatenate([code] * (tile // 16), axis=0)

    one, zero = jnp.ones((), BF16), jnp.zeros((), BF16)

    def send(slot_, to):
        pltpu.make_async_remote_copy(
            src_ref=snd.at[slot_],
            dst_ref=rcv.at[place],
            send_sem=ssem,
            recv_sem=rsem.at[mine_k],
            device_id=to,
            device_id_type=MESH,
        ).start()

    for g in range(groups):
        picks = jnp.concatenate(
            [
                jnp.where(lines == spread(code0, g), one, zero),
                jnp.where(lines == spread(code1, g), one, zero),
            ],
            axis=0,
        )
        both = mm(picks, mel2[...])
        packed = jnp.where(low, both[:tile], both[tile:]).astype(BF16)
        snd[g * G : g * G + G] = packed.reshape(G, 8, 128)

    pl.semaphore_wait(barrier, devices - 1)
    for j in range(groups):
        each_peer(j, rem(mine_k + j, groups), send)
    rcv[pl.ds(place, 1)] = snd[pl.ds(place, 1)]

    for load in loads[3:]:
        load.wait()
    r4 = iota((16, width), 0)
    states = mm(conv_ref[...], w_state_ref[...])
    tiled = jnp.zeros((16, width), F32)
    for s in range(sess):
        tiled = jnp.where(r4 % 4 == s, states[s : s + 1, :], tiled)
    hi = tiled.astype(BF16).astype(F32)
    mid = (tiled - hi).astype(BF16).astype(F32)
    lo = tiled - hi - mid
    terms = jnp.where(r4 < 4, hi, jnp.where(r4 < 8, mid, jnp.where(r4 < 12, lo, 0.0)))
    lanes4 = jnp.where((iota((16, width), 1) // 64 == r4) & (r4 < 4), 1.0, 0.0)
    lengths = [lens_ref[me * sess + s] for s in range(sess)]
    wx[...] = jnp.zeros_like(wx)
    wx[0:mel, 0:width] = w_in_ref[...]
    wx[mel : mel + 16, :] = jnp.concatenate([terms, lanes4], axis=1).astype(BF16)
    lane = iota((1, width), 1)
    past = jnp.zeros((1, width), F32)
    for s in range(sess):
        past = jnp.where(lane == 64 * s, (window - lengths[s]).astype(F32), past)

    low_w = iota((width, 128), 1) < 64
    for pair in range(HEADS // 2):
        w = w_qkv_ref[:, pair * 128 : pair * 128 + 128].astype(F32) * 0.125
        turned = pltpu.roll(w, 64, 1)
        wq[:, pair * 256 : pair * 256 + 128] = jnp.where(low_w, w, turned).astype(BF16)
        wq[:, pair * 256 + 128 : pair * 256 + 256] = jnp.where(low_w, turned, w).astype(BF16)
    wq[:, 2 * width :] = w_qkv_ref[:, width:]

    kv_copy.wait()
    low_p = iota((window, 128), 1) < 64
    row_p = iota((window, 128), 0)

    def turn(a, by):
        return jnp.concatenate([a[window - by :], a[: window - by]], axis=0) if by else a

    for sp in range(2):
        there = slice(sp * 128, sp * 128 + 128)
        in_one = row_p < lengths[2 * sp]
        in_two = row_p < lengths[2 * sp + 1]
        for pair in range(HEADS // 2):
            cols = slice(pair * 128, pair * 128 + 128)
            for which in range(2):
                one_ = kvb[2 * sp, which, :, cols].astype(F32)
                two_ = kvb[2 * sp + 1, which, :, cols].astype(F32)
                if which == 0:
                    one_ = jnp.where(in_one, one_, one_[0:1, :])
                    two_ = jnp.where(in_two, two_, two_[0:1, :])
                else:
                    one_ = jnp.where(in_one, one_, 0.0)
                    two_ = jnp.where(in_two, two_, 0.0)
                one_ = turn(one_, 64 * (2 * sp))
                two_ = turn(two_, 64 * (2 * sp + 1))
                even = jnp.where(low_p, one_, pltpu.roll(two_, 64, 1)).astype(BF16)
                odd = jnp.where(low_p, pltpu.roll(one_, 64, 1), two_).astype(BF16)
                if which == 0:
                    kt[2 * pair, there, :] = even.T
                    kt[2 * pair + 1, there, :] = odd.T
                else:
                    vc[2 * pair, :, there] = even
                    vc[2 * pair + 1, :, there] = odd

    total = 12 * G
    sums[...] = jnp.zeros_like(sums)
    counts[...] = jnp.zeros_like(counts)
    pick = one_hot(
        (iota((4 * G, 8 * G), 0) // 4 == iota((4 * G, 8 * G), 1) // 8)
        & (iota((4 * G, 8 * G), 0) % 4 == iota((4 * G, 8 * G), 1) % 8)
    )
    slot_lane = one_hot((iota((8, 128), 1) == iota((8, 128), 0) + mel) & (iota((8, 128), 0) < sess))
    low_r = iota((total, 128), 1) < 64
    sub = iota((G // 2, 8, 128), 1) < 4

    def arrive(j):
        g = rem(mine_k + groups - j, groups)
        part = rcv.at[pl.ds(g * G, G if j else G - 1)]
        pltpu.make_async_copy(part, part, rsem.at[g]).wait()

    def front(j):
        g = rem(mine_k + groups - j, groups)
        a = rcv[pl.ds(g * G, G)].reshape(8 * G, 128)
        x = pltpu.roll(mm(pick, a), 64, 1).astype(BF16)
        both = jnp.concatenate([a, x], axis=0)
        f = mm(both, wx[...])
        pre = f[:, :width]
        hidden = (pre * jax.nn.sigmoid(pre)).astype(BF16)
        marks[j % 2] = both
        lanes[j % 2] = f[:, width:]
        masks[j % 2] = f[:, width:].astype(BF16)
        kept[j % 2] = 1.0 - f[:, width:] * past
        hid[j % 2] = hidden
        qkv = mm(hidden, wq[...])
        qkvs[j % 2, :, : 2 * width] = qkv[:, : 2 * width] * LOG2E
        qkvs[j % 2, :, 2 * width :] = qkv[:, 2 * width :]

    def heads(j):
        g = rem(mine_k + groups - j, groups)
        qkv = qkvs.at[j % 2]
        b = j % 2
        outs = []
        for pair in range(HEADS // 2):
            kcol = 2 * width + pair * 128
            k = qkv[:, kcol : kcol + 128]
            v = qkv[:, kcol + width : kcol + width + 128]
            mixed, tops, totals, qs = [], [], [], []
            for h in range(2):
                at = pair * 256 + h * 128
                qs.append(qkv[:, at : at + 128])
                q = qs[h].astype(BF16)
                wide = jnp.concatenate([q, q], axis=1) * masks[b]
                raw[h] = mm(wide, kt[2 * pair + h])
                top = jnp.max(raw[h], axis=1, keepdims=True)
                e = jnp.exp2(raw[h] - top)
                expo[h] = e.astype(BF16)
                part = (e[:, :128] * kept[b, :, :128] + e[:, 128:256] * kept[b, :, 128:]) + (
                    e[:, 256:384] + e[:, 384:]
                )
                totals.append(jnp.sum(part, axis=1, keepdims=True))
                tops.append(top)
                o = mm(expo[h], vc[2 * pair + h])
                mixed.append(o[:, :128] * lanes[b, :, :128] + o[:, 128:] * lanes[b, :, 128:])
            mix = jnp.where(low_r, mixed[0], mixed[1]) + pltpu.roll(
                jnp.where(low_r, mixed[1], mixed[0]), 64, 1
            )
            top = jnp.where(low_r, tops[0], tops[1])
            tot = jnp.where(low_r, totals[0], totals[1])
            prod = jnp.where(low_r, qs[0], qs[1]) * k
            own0 = jnp.sum(jnp.where(low_r, prod, 0.0), axis=1, keepdims=True)
            own1 = jnp.sum(jnp.where(low_r, 0.0, prod), axis=1, keepdims=True)
            mine = jnp.where(low_r, own0, own1)
            peak = jnp.maximum(top, mine)
            ea = jnp.exp2(top - peak)
            eb = jnp.exp2(mine - peak)
            outs.append(((ea * mix + eb * v) / (ea * tot + eb)).astype(BF16))
        if j + 1 < groups:
            front(j + 1)
        attn = jnp.concatenate(outs, axis=1)
        scored = (hid[b].astype(F32) + mm(attn, w_out_ref[...])).astype(BF16)
        wide = scored.astype(F32)
        first = pl.ds(g * G, G)
        rsnd[first, 0:8, :] = scored[: 8 * G, :128].reshape(G, 8, 128)
        rsnd[first, 8:16, :] = scored[: 8 * G, 128:].reshape(G, 8, 128)
        left = wide[8 * G :, :128].reshape(G // 2, 8, 128)
        right = wide[8 * G :, 128:].reshape(G // 2, 8, 128)
        ones = jnp.where(sub, left, pltpu.roll(right, 4, 1))
        twos = jnp.where(sub, pltpu.roll(left, 4, 1), right)
        rsnd[first, 16:24, :] = jnp.stack([ones, twos], axis=1).reshape(G, 8, 128).astype(BF16)

        def back(slot_, to):
            pltpu.make_async_remote_copy(
                src_ref=rsnd.at[slot_],
                dst_ref=ret.at[place],
                send_sem=bsem,
                recv_sem=csem.at[mine_k],
                device_id=to,
                device_id_type=MESH,
            ).start()

        each_peer(j, g, back)
        hits = lax.dot_general(
            slot_lane, marks[j % 2], (((1,), (1,)), ((), ())), preferred_element_type=F32
        )
        sums[...] += mm(hits.astype(BF16), scored)
        counts[...] += jnp.sum(hits, axis=1, keepdims=True)

    arrive(0)
    front(0)
    for j in range(groups):
        if j + 1 < groups:
            arrive(j + 1)
        heads(j)
    ret[pl.ds(place, 1)] = rsnd[pl.ds(place, 1)]

    diag = iota((128, 128), 0) == iota((128, 128), 1)
    for b in range(rows // 128):
        here = slice(b * 128, b * 128 + 128)
        c0 = jnp.sum(jnp.where(diag, code0[:, here].astype(F32), 0.0), axis=1, keepdims=True)
        c2 = jnp.sum(jnp.where(diag, code2[:, here].astype(F32), 0.0), axis=1, keepdims=True)
        across = iota((128, 256), 1).astype(F32).astype(BF16)
        for t in range(devices * 8 // 256):
            near = jnp.broadcast_to(c0 - t * 256, (128, 256)).astype(BF16)
            um[here, t * 256 : t * 256 + 256] = jnp.where(across == near, one, zero)
        for t in range(devices * 4 // 256):
            near = jnp.broadcast_to(c2 - t * 256, (128, 256)).astype(BF16)
            ue[here, t * 256 : t * 256 + 256] = jnp.where(across == near, one, zero)

    n = counts[0:sess, 0:1]
    mean = sums[0:sess, :] / jnp.maximum(n, 1.0)
    updated = jnp.where(n > 0, mean, conv_ref[...].astype(F32)).astype(BF16).astype(F32)
    upd_out[...] = jnp.zeros_like(upd_out)
    upd_out[0:sess, :] = updated
    push = pltpu.make_async_remote_copy(
        src_ref=upd_out,
        dst_ref=upd_in,
        send_sem=usem.at[0],
        recv_sem=usem.at[1],
        device_id=(ing, lax.rem(own + 1, n_own)),
        device_id_type=MESH,
    )
    push.start()
    sub = iota((G // 2, 8, 128), 1) < 4

    def unpack(j, c):
        k = (mine_k + j) % groups

        @pl.when(j == 0)
        def _():
            part = ret.at[pl.ds(k * G, G - 1)]
            pltpu.make_async_copy(part, part, csem.at[k]).wait()

        @pl.when(j > 0)
        def _():
            part = ret.at[pl.ds(k * G, G)]
            pltpu.make_async_copy(part, part, csem.at[k]).wait()

        here = pl.ds(k * G, G)
        main = jnp.concatenate(
            [
                ret[here, 0:8, :].reshape(G * 8, 128),
                ret[here, 8:16, :].reshape(G * 8, 128),
            ],
            axis=1,
        )
        extra = ret[here, 16:24, :].astype(F32).reshape(G // 2, 2, 8, 128)
        ones, twos = extra[:, 0], extra[:, 1]
        left = jnp.where(sub, ones, pltpu.roll(twos, 4, 1)).reshape(G * 4, 128)
        right = jnp.where(sub, pltpu.roll(ones, 4, 1), twos).reshape(G * 4, 128)
        extra = jnp.concatenate([left, right], axis=1).astype(BF16)
        mains = um[:, pl.ds(pl.multiple_of(k * (G * 8), 256), G * 8)]
        extras = ue[:, pl.ds(pl.multiple_of(k * (G * 4), 128), G * 4)]
        more = mm(mains, main) + mm(extras, extra)

        @pl.when(j == 0)
        def _():
            acc[...] = more

        @pl.when((j > 0) & (j < groups - 1))
        def _():
            acc[...] += more

        @pl.when(j == groups - 1)
        def _():
            out_ref[...] = (acc[...] + more).astype(BF16)

        return c

    lax.fori_loop(0, groups, unpack, 0)
    other = snd.at[pl.ds(0, devices - 1)]
    pltpu.make_async_copy(other, other, ssem).wait()
    other = rsnd.at[pl.ds(0, devices - 1)]
    pltpu.make_async_copy(other, other, bsem).wait()
    push.wait()
    r8 = iota((8, width), 0)
    prev = ing * n_own + lax.rem(own + n_own - 1, n_own)
    keep = (r8 < sess) & (r8 < sess - mig_ref[me])
    live = (r8 >= sess) & (r8 - sess >= MIG - mig_ref[prev])
    table = jnp.where(
        keep, upd_out[...], jnp.where(live, pltpu.roll(upd_in[...], MIG, 0), 0.0)
    ).astype(BF16)
    new_ref[...] = table[0 : sess + MIG, :]


def body(
    frame_mel,
    row_device,
    row_slot,
    window_length,
    migrate_count,
    conv_state,
    kv_cache,
    w_in,
    w_state,
    w_qkv,
    w_out,
):
    n_ing = lax.axis_size("ingest")
    n_own = lax.axis_size("owner")
    devices = n_ing * n_own
    rows, mel = frame_mel.shape
    sess, _, window, width = kv_cache.shape
    G = n_own
    groups = devices // G
    vmem = pl.BlockSpec(memory_space=pltpu.VMEM)
    return pl.pallas_call(
        functools.partial(kernel, n_ing, n_own, G),
        out_shape=(
            jax.ShapeDtypeStruct((rows, width), BF16),
            jax.ShapeDtypeStruct((sess + MIG, width), BF16),
        ),
        in_specs=[pl.BlockSpec(memory_space=pltpu.HBM)] * 11,
        out_specs=(vmem, vmem),
        scratch_shapes=[
            pltpu.VMEM((1, rows), I32),
            pltpu.VMEM((1, rows), I32),
            pltpu.SMEM(window_length.shape, I32),
            pltpu.SMEM(migrate_count.shape, I32),
            pltpu.VMEM(conv_state.shape, BF16),
            pltpu.VMEM((mel, rows), BF16),
            pltpu.VMEM(w_in.shape, BF16),
            pltpu.VMEM(w_state.shape, BF16),
            pltpu.VMEM(w_qkv.shape, BF16),
            pltpu.VMEM(w_out.shape, BF16),
            pltpu.VMEM((devices, 8, 128), BF16),
            pltpu.VMEM((devices, 8, 128), BF16),
            pltpu.VMEM((devices, 24, 128), BF16),
            pltpu.VMEM((devices, 24, 128), BF16),
            pltpu.VMEM(kv_cache.shape, BF16),
            pltpu.VMEM((HEADS, width, window), BF16),
            pltpu.VMEM((HEADS, window, width), BF16),
            pltpu.VMEM((rows, 128), BF16),
            pltpu.VMEM((rows, devices * 8), BF16),
            pltpu.VMEM((rows, devices * 4), BF16),
            pltpu.VMEM((128, 2 * width), BF16),
            pltpu.VMEM((width, 4 * width), BF16),
            pltpu.VMEM((8, width), F32),
            pltpu.VMEM((8, 128), F32),
            pltpu.VMEM((8, width), F32),
            pltpu.VMEM((8, width), F32),
            pltpu.VMEM((rows, width), F32),
            pltpu.VMEM((2, 12 * G, 128), BF16),
            pltpu.VMEM((2, 12 * G, window), F32),
            pltpu.VMEM((2, 12 * G, window), BF16),
            pltpu.VMEM((2, 12 * G, width), F32),
            pltpu.VMEM((2, 12 * G, width), BF16),
            pltpu.VMEM((2, 12 * G, width), F32),
            pltpu.VMEM((2, 12 * G, width), BF16),
            pltpu.VMEM((2, 12 * G, 4 * width), F32),
            pltpu.SemaphoreType.DMA,
            pltpu.SemaphoreType.DMA,
            pltpu.SemaphoreType.DMA((groups,)),
            pltpu.SemaphoreType.DMA,
            pltpu.SemaphoreType.DMA((groups,)),
            pltpu.SemaphoreType.DMA((2,)),
            pltpu.SemaphoreType.DMA((10,)),
        ],
        compiler_params=pltpu.CompilerParams(
            collective_id=0, has_side_effects=True, vmem_limit_bytes=40 << 20
        ),
        name="scorer",
    )(
        *(
            pltpu.with_memory_space_constraint(a, pltpu.HBM)
            for a in (
                row_device.reshape(1, rows),
                row_slot.reshape(1, rows),
                window_length,
                migrate_count,
                conv_state,
                frame_mel.T,
                kv_cache,
                w_in,
                w_state,
                w_qkv,
                w_out,
            )
        )
    )


def solution(mesh):
    placed = (
        P(("ingest", "owner"), None),
        P(("ingest", "owner"), None),
        P(("ingest", "owner")),
        P(),
        P(),
        P(("ingest", "owner"), None),
        P(("ingest", "owner"), None, None, None),
        P(),
        P(),
        P(),
        P(),
    )
    return jax.shard_map(
        body,
        mesh=mesh,
        in_specs=placed,
        out_specs=(P(("ingest", "owner"), None), P(("ingest", "owner"), None)),
        check_vma=False,
    )
```

```python
import functools

import jax
import jax.numpy as jnp
from jax import lax
from jax.experimental import pallas as pl
from jax.experimental.pallas import tpu as pltpu
from jax.sharding import PartitionSpec as P

HEADS = 4
MIG = 2
LOG2E = 1.4426950408889634
MESH = pl.DeviceIdType.MESH
F32 = jnp.float32
BF16 = jnp.bfloat16
I32 = jnp.int32


def iota(shape, dim):
    return lax.broadcasted_iota(I32, shape, dim)


def one_hot(mask):
    return jnp.where(mask, 1.0, 0.0).astype(BF16)


def mm(a, b):
    return jnp.dot(a, b, preferred_element_type=F32)


def kernel(
    n_ing,
    n_own,
    G,
    dev_hbm,
    slot_hbm,
    lens_hbm,
    mig_hbm,
    conv_hbm,
    mel_hbm,
    kv_ref,
    w_in_hbm,
    w_state_hbm,
    w_qkv_hbm,
    w_out_hbm,
    out_ref,
    new_ref,
    dev_ref,
    slot_ref,
    lens_ref,
    mig_ref,
    conv_ref,
    mel_ref,
    w_in_ref,
    w_state_ref,
    w_qkv_ref,
    w_out_ref,
    snd,
    rcv,
    rsnd,
    ret,
    kvb,
    kt,
    vc,
    mel2,
    um,
    ue,
    wx,
    wq,
    sums,
    counts,
    upd_out,
    upd_in,
    acc,
    marks,
    raw,
    expo,
    lanes,
    masks,
    kept,
    hid,
    qkvs,
    kv_sem,
    ssem,
    rsem,
    bsem,
    csem,
    usem,
    in_sem,
):
    devices = n_ing * n_own
    groups = devices // G
    rows = mel_ref.shape[1]
    mel = mel_ref.shape[0]
    sess, width = conv_ref.shape
    window = kv_ref.shape[2]
    ing = lax.axis_index("ingest")
    own = lax.axis_index("owner")
    me = ing * n_own + own

    N = n_ing
    rem = lax.rem
    yy, zz, core = lax.div(own, 2 * N), rem(lax.div(own, 2), N), rem(own, 2)
    mine_k = rem(ing + yy + zz, N)
    place = mine_k * G + ing * (2 * N) + yy * 2 + core

    def peer(k, dx, dy, dc):
        x, y, c = rem(ing + dx, N), rem(yy + dy, N), rem(core + dc, 2)
        z = rem(k + 2 * N - x - y, N)
        return k * G + x * (2 * N) + y * 2 + c, (x, y * (2 * N) + z * 2 + c)

    def each_peer(j, k, start):
        def step(dx, c):
            for dy in range(N):
                for dc in range(2):
                    if dy + dc > 0:
                        start(*peer(k, dx, dy, dc))
            return c

        lax.fori_loop(0, N, step, 0)
        for dx in range(1, N):
            start(*peer(k, dx, 0, 0))
        if j > 0:
            start(*peer(k, 0, 0, 0))

    pairs = [
        (dev_hbm, dev_ref),
        (slot_hbm, slot_ref),
        (mel_hbm, mel_ref),
        (lens_hbm, lens_ref),
        (conv_hbm, conv_ref),
        (w_state_hbm, w_state_ref),
        (w_in_hbm, w_in_ref),
        (w_qkv_hbm, w_qkv_ref),
        (w_out_hbm, w_out_ref),
        (mig_hbm, mig_ref),
    ]
    loads = [pltpu.make_async_copy(a, b, in_sem.at[i]) for i, (a, b) in enumerate(pairs)]
    for load in loads:
        load.start()
    kv_copy = pltpu.make_async_copy(kv_ref, kvb, kv_sem)
    kv_copy.start()

    barrier = pltpu.get_barrier_semaphore()

    def greet(i, c):
        for a in range(n_ing):
            x = lax.rem(ing + a, n_ing)
            y = lax.rem(own + i, n_own)
            pl.semaphore_signal(barrier, inc=1, device_id=(x, y), device_id_type=MESH)
        return c

    lax.fori_loop(1, n_own, greet, 0, unroll=4)
    for a in range(1, n_ing):
        x = lax.rem(ing + a, n_ing)
        pl.semaphore_signal(barrier, inc=1, device_id=(x, own), device_id_type=MESH)

    for load in loads[:3]:
        load.wait()
    dev = dev_ref[...]
    slot = slot_ref[...]
    step = 256
    upper = one_hot(iota((step, step), 0) < iota((step, step), 1))
    lane_dev = iota((devices, step), 0)
    carry = jnp.zeros((devices, 1), F32)
    ranks = []
    for b in range(rows // step):
        hit = jnp.where(lane_dev == dev[:, b * step : (b + 1) * step], 1.0, 0.0)
        before = mm(hit.astype(BF16), upper) + carry
        ranks.append(jnp.sum(before * hit, axis=0, keepdims=True))
        carry = carry + jnp.sum(hit, axis=1, keepdims=True)
    rank = jnp.concatenate(ranks, axis=1).astype(I32)
    x, y, z = dev // n_own, (dev // (2 * N)) % N, (dev // 2) % N
    spot = (x + y + z) % N * G + x * (2 * N) + y * 2 + dev % 2
    code0 = jnp.where(rank < 8, spot * 8 + rank, -1)
    code1 = jnp.where(rank >= 8, spot * 8 + rank - 8, -1)
    code2 = jnp.where(rank >= 8, spot * 4 + rank - 8, -1)

    r16 = iota((16, rows), 0)
    slots = one_hot((r16 % 4 == slot) & (r16 < 12))
    half = jnp.concatenate([mel_ref[...], slots], axis=0)
    mel2[...] = jnp.concatenate([half, half], axis=0).T

    tile = G * 8
    low = iota((tile, 128), 1) < 64
    lines = jnp.concatenate([iota((tile, 128), 0).astype(F32).astype(BF16)] * (rows // 128), axis=1)

    def spread(code, g):
        code = jnp.broadcast_to((code - g * tile).astype(F32), (16, rows)).astype(BF16)
        return jnp.concatenate([code] * (tile // 16), axis=0)

    one, zero = jnp.ones((), BF16), jnp.zeros((), BF16)

    def send(slot_, to):
        pltpu.make_async_remote_copy(
            src_ref=snd.at[slot_],
            dst_ref=rcv.at[place],
            send_sem=ssem,
            recv_sem=rsem.at[mine_k],
            device_id=to,
            device_id_type=MESH,
        ).start()

    def pack(j):
        g = rem(mine_k + j, groups)
        picks = jnp.concatenate(
            [
                jnp.where(lines == spread(code0, g), one, zero),
                jnp.where(lines == spread(code1, g), one, zero),
            ],
            axis=0,
        )
        both = mm(picks, mel2[...])
        packed = jnp.where(low, both[:tile], both[tile:]).astype(BF16)
        snd[pl.ds(g * G, G)] = packed.reshape(G, 8, 128)

    pack(0)
    pack(1)
    pl.semaphore_wait(barrier, devices - 1)
    each_peer(0, mine_k, send)
    each_peer(1, rem(mine_k + 1, groups), send)
    for j in range(2, groups):
        pack(j)
        each_peer(j, rem(mine_k + j, groups), send)
    rcv[pl.ds(place, 1)] = snd[pl.ds(place, 1)]

    for load in loads[3:]:
        load.wait()
    r4 = iota((16, width), 0)
    states = mm(conv_ref[...], w_state_ref[...])
    tiled = jnp.zeros((16, width), F32)
    for s in range(sess):
        tiled = jnp.where(r4 % 4 == s, states[s : s + 1, :], tiled)
    hi = tiled.astype(BF16).astype(F32)
    mid = (tiled - hi).astype(BF16).astype(F32)
    lo = tiled - hi - mid
    terms = jnp.where(r4 < 4, hi, jnp.where(r4 < 8, mid, jnp.where(r4 < 12, lo, 0.0)))
    lanes4 = jnp.where((iota((16, width), 1) // 64 == r4) & (r4 < 4), 1.0, 0.0)
    lengths = [lens_ref[me * sess + s] for s in range(sess)]
    wx[...] = jnp.zeros_like(wx)
    wx[0:mel, 0:width] = w_in_ref[...]
    wx[mel : mel + 16, :] = jnp.concatenate([terms, lanes4], axis=1).astype(BF16)
    lane = iota((1, width), 1)
    past = jnp.zeros((1, width), F32)
    for s in range(sess):
        past = jnp.where(lane == 64 * s, (window - lengths[s]).astype(F32), past)

    low_w = iota((width, 128), 1) < 64
    for pair in range(HEADS // 2):
        w = w_qkv_ref[:, pair * 128 : pair * 128 + 128].astype(F32) * 0.125
        turned = pltpu.roll(w, 64, 1)
        wq[:, pair * 256 : pair * 256 + 128] = jnp.where(low_w, w, turned).astype(BF16)
        wq[:, pair * 256 + 128 : pair * 256 + 256] = jnp.where(low_w, turned, w).astype(BF16)
    wq[:, 2 * width :] = w_qkv_ref[:, width:]

    kv_copy.wait()
    low_p = iota((window, 128), 1) < 64
    row_p = iota((window, 128), 0)

    def turn(a, by):
        return jnp.concatenate([a[window - by :], a[: window - by]], axis=0) if by else a

    for sp in range(2):
        there = slice(sp * 128, sp * 128 + 128)
        in_one = row_p < lengths[2 * sp]
        in_two = row_p < lengths[2 * sp + 1]
        for pair in range(HEADS // 2):
            cols = slice(pair * 128, pair * 128 + 128)
            for which in range(2):
                one_ = kvb[2 * sp, which, :, cols].astype(F32)
                two_ = kvb[2 * sp + 1, which, :, cols].astype(F32)
                if which == 0:
                    one_ = jnp.where(in_one, one_, one_[0:1, :])
                    two_ = jnp.where(in_two, two_, two_[0:1, :])
                else:
                    one_ = jnp.where(in_one, one_, 0.0)
                    two_ = jnp.where(in_two, two_, 0.0)
                one_ = turn(one_, 64 * (2 * sp))
                two_ = turn(two_, 64 * (2 * sp + 1))
                even = jnp.where(low_p, one_, pltpu.roll(two_, 64, 1)).astype(BF16)
                odd = jnp.where(low_p, pltpu.roll(one_, 64, 1), two_).astype(BF16)
                if which == 0:
                    kt[2 * pair, there, :] = even.T
                    kt[2 * pair + 1, there, :] = odd.T
                else:
                    vc[2 * pair, :, there] = even
                    vc[2 * pair + 1, :, there] = odd

    total = 12 * G
    sums[...] = jnp.zeros_like(sums)
    counts[...] = jnp.zeros_like(counts)
    pick = one_hot(
        (iota((4 * G, 8 * G), 0) // 4 == iota((4 * G, 8 * G), 1) // 8)
        & (iota((4 * G, 8 * G), 0) % 4 == iota((4 * G, 8 * G), 1) % 8)
    )
    slot_lane = one_hot((iota((8, 128), 1) == iota((8, 128), 0) + mel) & (iota((8, 128), 0) < sess))
    low_r = iota((total, 128), 1) < 64
    sub = iota((G // 2, 8, 128), 1) < 4

    def arrive(j):
        g = rem(mine_k + groups - j, groups)
        part = rcv.at[pl.ds(g * G, G if j else G - 1)]
        pltpu.make_async_copy(part, part, rsem.at[g]).wait()

    def front(j):
        g = rem(mine_k + groups - j, groups)
        a = rcv[pl.ds(g * G, G)].reshape(8 * G, 128)
        x = pltpu.roll(mm(pick, a), 64, 1).astype(BF16)
        both = jnp.concatenate([a, x], axis=0)
        f = mm(both, wx[...])
        pre = f[:, :width]
        hidden = (pre * jax.nn.sigmoid(pre)).astype(BF16)
        marks[j % 2] = both
        lanes[j % 2] = f[:, width:]
        masks[j % 2] = f[:, width:].astype(BF16)
        kept[j % 2] = 1.0 - f[:, width:] * past
        hid[j % 2] = hidden
        qkv = mm(hidden, wq[...])
        qkvs[j % 2, :, : 2 * width] = qkv[:, : 2 * width] * LOG2E
        qkvs[j % 2, :, 2 * width :] = qkv[:, 2 * width :]

    def heads(j):
        g = rem(mine_k + groups - j, groups)
        qkv = qkvs.at[j % 2]
        b = j % 2
        outs = []
        for pair in range(HEADS // 2):
            kcol = 2 * width + pair * 128
            k = qkv[:, kcol : kcol + 128]
            v = qkv[:, kcol + width : kcol + width + 128]
            mixed, tops, totals, qs = [], [], [], []
            for h in range(2):
                at = pair * 256 + h * 128
                qs.append(qkv[:, at : at + 128])
                q = qs[h].astype(BF16)
                wide = jnp.concatenate([q, q], axis=1) * masks[b]
                raw[h] = mm(wide, kt[2 * pair + h])
                top = jnp.max(raw[h], axis=1, keepdims=True)
                e = jnp.exp2(raw[h] - top)
                expo[h] = e.astype(BF16)
                part = (e[:, :128] * kept[b, :, :128] + e[:, 128:256] * kept[b, :, 128:]) + (
                    e[:, 256:384] + e[:, 384:]
                )
                totals.append(jnp.sum(part, axis=1, keepdims=True))
                tops.append(top)
                o = mm(expo[h], vc[2 * pair + h])
                mixed.append(o[:, :128] * lanes[b, :, :128] + o[:, 128:] * lanes[b, :, 128:])
            mix = jnp.where(low_r, mixed[0], mixed[1]) + pltpu.roll(
                jnp.where(low_r, mixed[1], mixed[0]), 64, 1
            )
            top = jnp.where(low_r, tops[0], tops[1])
            tot = jnp.where(low_r, totals[0], totals[1])
            prod = jnp.where(low_r, qs[0], qs[1]) * k
            own0 = jnp.sum(jnp.where(low_r, prod, 0.0), axis=1, keepdims=True)
            own1 = jnp.sum(jnp.where(low_r, 0.0, prod), axis=1, keepdims=True)
            mine = jnp.where(low_r, own0, own1)
            peak = jnp.maximum(top, mine)
            ea = jnp.exp2(top - peak)
            eb = jnp.exp2(mine - peak)
            outs.append(((ea * mix + eb * v) / (ea * tot + eb)).astype(BF16))
        if j + 1 < groups:
            front(j + 1)
        attn = jnp.concatenate(outs, axis=1)
        scored = (hid[b].astype(F32) + mm(attn, w_out_ref[...])).astype(BF16)
        wide = scored.astype(F32)
        first = pl.ds(g * G, G)
        rsnd[first, 0:8, :] = scored[: 8 * G, :128].reshape(G, 8, 128)
        rsnd[first, 8:16, :] = scored[: 8 * G, 128:].reshape(G, 8, 128)
        left = wide[8 * G :, :128].reshape(G // 2, 8, 128)
        right = wide[8 * G :, 128:].reshape(G // 2, 8, 128)
        ones = jnp.where(sub, left, pltpu.roll(right, 4, 1))
        twos = jnp.where(sub, pltpu.roll(left, 4, 1), right)
        rsnd[first, 16:24, :] = jnp.stack([ones, twos], axis=1).reshape(G, 8, 128).astype(BF16)

        def back(slot_, to):
            pltpu.make_async_remote_copy(
                src_ref=rsnd.at[slot_],
                dst_ref=ret.at[place],
                send_sem=bsem,
                recv_sem=csem.at[mine_k],
                device_id=to,
                device_id_type=MESH,
            ).start()

        each_peer(j, g, back)
        hits = lax.dot_general(
            slot_lane, marks[j % 2], (((1,), (1,)), ((), ())), preferred_element_type=F32
        )
        sums[...] += mm(hits.astype(BF16), scored)
        counts[...] += jnp.sum(hits, axis=1, keepdims=True)

    arrive(0)
    front(0)
    for j in range(groups):
        if j + 1 < groups:
            arrive(j + 1)
        heads(j)
    ret[pl.ds(place, 1)] = rsnd[pl.ds(place, 1)]

    diag = iota((128, 128), 0) == iota((128, 128), 1)
    for b in range(rows // 128):
        here = slice(b * 128, b * 128 + 128)
        c0 = jnp.sum(jnp.where(diag, code0[:, here].astype(F32), 0.0), axis=1, keepdims=True)
        c2 = jnp.sum(jnp.where(diag, code2[:, here].astype(F32), 0.0), axis=1, keepdims=True)
        across = iota((128, 256), 1).astype(F32).astype(BF16)
        for t in range(devices * 8 // 256):
            near = jnp.broadcast_to(c0 - t * 256, (128, 256)).astype(BF16)
            um[here, t * 256 : t * 256 + 256] = jnp.where(across == near, one, zero)
        for t in range(devices * 4 // 256):
            near = jnp.broadcast_to(c2 - t * 256, (128, 256)).astype(BF16)
            ue[here, t * 256 : t * 256 + 256] = jnp.where(across == near, one, zero)

    n = counts[0:sess, 0:1]
    mean = sums[0:sess, :] / jnp.maximum(n, 1.0)
    updated = jnp.where(n > 0, mean, conv_ref[...].astype(F32)).astype(BF16).astype(F32)
    upd_out[...] = jnp.zeros_like(upd_out)
    upd_out[0:sess, :] = updated
    push = pltpu.make_async_remote_copy(
        src_ref=upd_out,
        dst_ref=upd_in,
        send_sem=usem.at[0],
        recv_sem=usem.at[1],
        device_id=(ing, lax.rem(own + 1, n_own)),
        device_id_type=MESH,
    )
    push.start()
    sub = iota((G // 2, 8, 128), 1) < 4

    def unpack(j, c):
        k = (mine_k + j) % groups

        @pl.when(j == 0)
        def _():
            part = ret.at[pl.ds(k * G, G - 1)]
            pltpu.make_async_copy(part, part, csem.at[k]).wait()

        @pl.when(j > 0)
        def _():
            part = ret.at[pl.ds(k * G, G)]
            pltpu.make_async_copy(part, part, csem.at[k]).wait()

        here = pl.ds(k * G, G)
        main = jnp.concatenate(
            [
                ret[here, 0:8, :].reshape(G * 8, 128),
                ret[here, 8:16, :].reshape(G * 8, 128),
            ],
            axis=1,
        )
        extra = ret[here, 16:24, :].astype(F32).reshape(G // 2, 2, 8, 128)
        ones, twos = extra[:, 0], extra[:, 1]
        left = jnp.where(sub, ones, pltpu.roll(twos, 4, 1)).reshape(G * 4, 128)
        right = jnp.where(sub, pltpu.roll(ones, 4, 1), twos).reshape(G * 4, 128)
        extra = jnp.concatenate([left, right], axis=1).astype(BF16)
        mains = um[:, pl.ds(pl.multiple_of(k * (G * 8), 256), G * 8)]
        extras = ue[:, pl.ds(pl.multiple_of(k * (G * 4), 128), G * 4)]
        more = mm(mains, main) + mm(extras, extra)

        @pl.when(j == 0)
        def _():
            acc[...] = more

        @pl.when((j > 0) & (j < groups - 1))
        def _():
            acc[...] += more

        @pl.when(j == groups - 1)
        def _():
            out_ref[...] = (acc[...] + more).astype(BF16)

        return c

    lax.fori_loop(0, groups, unpack, 0)
    other = snd.at[pl.ds(0, devices - 1)]
    pltpu.make_async_copy(other, other, ssem).wait()
    other = rsnd.at[pl.ds(0, devices - 1)]
    pltpu.make_async_copy(other, other, bsem).wait()
    push.wait()
    r8 = iota((8, width), 0)
    prev = ing * n_own + lax.rem(own + n_own - 1, n_own)
    keep = (r8 < sess) & (r8 < sess - mig_ref[me])
    live = (r8 >= sess) & (r8 - sess >= MIG - mig_ref[prev])
    table = jnp.where(
        keep, upd_out[...], jnp.where(live, pltpu.roll(upd_in[...], MIG, 0), 0.0)
    ).astype(BF16)
    new_ref[...] = table[0 : sess + MIG, :]


def body(
    frame_mel,
    row_device,
    row_slot,
    window_length,
    migrate_count,
    conv_state,
    kv_cache,
    w_in,
    w_state,
    w_qkv,
    w_out,
):
    n_ing = lax.axis_size("ingest")
    n_own = lax.axis_size("owner")
    devices = n_ing * n_own
    rows, mel = frame_mel.shape
    sess, _, window, width = kv_cache.shape
    G = n_own
    groups = devices // G
    vmem = pl.BlockSpec(memory_space=pltpu.VMEM)
    return pl.pallas_call(
        functools.partial(kernel, n_ing, n_own, G),
        out_shape=(
            jax.ShapeDtypeStruct((rows, width), BF16),
            jax.ShapeDtypeStruct((sess + MIG, width), BF16),
        ),
        in_specs=[pl.BlockSpec(memory_space=pltpu.HBM)] * 11,
        out_specs=(vmem, vmem),
        scratch_shapes=[
            pltpu.VMEM((1, rows), I32),
            pltpu.VMEM((1, rows), I32),
            pltpu.SMEM(window_length.shape, I32),
            pltpu.SMEM(migrate_count.shape, I32),
            pltpu.VMEM(conv_state.shape, BF16),
            pltpu.VMEM((mel, rows), BF16),
            pltpu.VMEM(w_in.shape, BF16),
            pltpu.VMEM(w_state.shape, BF16),
            pltpu.VMEM(w_qkv.shape, BF16),
            pltpu.VMEM(w_out.shape, BF16),
            pltpu.VMEM((devices, 8, 128), BF16),
            pltpu.VMEM((devices, 8, 128), BF16),
            pltpu.VMEM((devices, 24, 128), BF16),
            pltpu.VMEM((devices, 24, 128), BF16),
            pltpu.VMEM(kv_cache.shape, BF16),
            pltpu.VMEM((HEADS, width, window), BF16),
            pltpu.VMEM((HEADS, window, width), BF16),
            pltpu.VMEM((rows, 128), BF16),
            pltpu.VMEM((rows, devices * 8), BF16),
            pltpu.VMEM((rows, devices * 4), BF16),
            pltpu.VMEM((128, 2 * width), BF16),
            pltpu.VMEM((width, 4 * width), BF16),
            pltpu.VMEM((8, width), F32),
            pltpu.VMEM((8, 128), F32),
            pltpu.VMEM((8, width), F32),
            pltpu.VMEM((8, width), F32),
            pltpu.VMEM((rows, width), F32),
            pltpu.VMEM((2, 12 * G, 128), BF16),
            pltpu.VMEM((2, 12 * G, window), F32),
            pltpu.VMEM((2, 12 * G, window), BF16),
            pltpu.VMEM((2, 12 * G, width), F32),
            pltpu.VMEM((2, 12 * G, width), BF16),
            pltpu.VMEM((2, 12 * G, width), F32),
            pltpu.VMEM((2, 12 * G, width), BF16),
            pltpu.VMEM((2, 12 * G, 4 * width), F32),
            pltpu.SemaphoreType.DMA,
            pltpu.SemaphoreType.DMA,
            pltpu.SemaphoreType.DMA((groups,)),
            pltpu.SemaphoreType.DMA,
            pltpu.SemaphoreType.DMA((groups,)),
            pltpu.SemaphoreType.DMA((2,)),
            pltpu.SemaphoreType.DMA((10,)),
        ],
        compiler_params=pltpu.CompilerParams(
            collective_id=0, has_side_effects=True, vmem_limit_bytes=40 << 20
        ),
        name="scorer",
    )(
        *(
            pltpu.with_memory_space_constraint(a, pltpu.HBM)
            for a in (
                row_device.reshape(1, rows),
                row_slot.reshape(1, rows),
                window_length,
                migrate_count,
                conv_state,
                frame_mel.T,
                kv_cache,
                w_in,
                w_state,
                w_qkv,
                w_out,
            )
        )
    )


def solution(mesh):
    placed = (
        P(("ingest", "owner"), None),
        P(("ingest", "owner"), None),
        P(("ingest", "owner")),
        P(),
        P(),
        P(("ingest", "owner"), None),
        P(("ingest", "owner"), None, None, None),
        P(),
        P(),
        P(),
        P(),
    )
    return jax.shard_map(
        body,
        mesh=mesh,
        in_specs=placed,
        out_specs=(P(("ingest", "owner"), None), P(("ingest", "owner"), None)),
        check_vma=False,
    )
```
